128 devices in a mesh: req: 64 (over z_lo, x, y, core), kvh: 2 (over z_hi).
Axes of the slice: x: 4, y: 4, z: 4 (z_hi: 2, z_lo: 2; z = z_hi * 2 + z_lo), core: 2. Of those that a mesh axis runs over, the one named last changes fastest.
Arguments:
- queries: bfloat16 [64, 4, 8192], P('req', None, 'kvh'), may hold values from -42 to 42
- incoming_keys: bfloat16 [64, 4, 1024], P('req', None, 'kvh'), may hold values from -6 to 6
- incoming_values: bfloat16 [64, 4, 1024], P('req', None, 'kvh'), may hold values from -6 to 6
- system_prefix_keys: bfloat16 [8, 16384, 1024], P(None, 'req', 'kvh'), may hold values from -6 to 6
- system_prefix_values: bfloat16 [8, 16384, 1024], P(None, 'req', 'kvh'), may hold values from -6 to 6
- request_history_keys: bfloat16 [64, 2048, 1024], P('req', None, 'kvh'), may hold values from -6 to 6
- request_history_values: bfloat16 [64, 2048, 1024], P('req', None, 'kvh'), may hold values from -6 to 6
- kept: int32 [64, 8, 1024], P('req', 'kvh'), may hold values from 0 to 2047, as said below
- membership: int32 [64, 1], P('req'), may hold values from 0 to 7; in each aligned block of 64 rows (0 to 63, 64 to 127, ...) at most 16 rows name the same one
- out_weight: bfloat16 [8192, 8192], P('kvh', 'req'), may hold values from -0.0625 to 0.0625
Outputs:
- layer_out: bfloat16 [64, 4, 8192], P(None, None, 'req')
The draws below stay inside these ranges and needn't reach their ends.
Inputs may be any that keep to these rules, and one draw needn't show every extreme that they name: `membership`: no system prompt has more than 16 requests; some prompt has exactly 16. `kept`: the 1024 positions of one request and KV head are distinct.
All inputs are finite; a program needn't handle non-finite values.
Results may differ from the reference program's by a relative error of at most 0.0049.
Values may be sent and summed in bfloat16 or wider, within the bound.
No kernel may reach another device: no remote copies, remote signals or barrier semaphores. Data moves between devices by JAX's collectives and lax.ppermute only.
A program may use at most 128 MiB of HBM per device.

```python
import math
import jax
import jax.numpy as jnp
import numpy as np
from jax import lax

D = 8192
HQ = 64
KEY_VALUE_HEADS = 8
HEAD_WIDTH = 128
HEADS_PER_GROUP = 8
PROMPT_COUNT = 8
DECODE_STEPS = 4
PROMPT_PORTION = 256
HISTORY_LENGTH = 2048
KEPT_TOKENS = 1024
REQUEST_COUNT = 64
CAP = 16
PREFIX_LENGTH = 16384
N_REQ = 64


def draw_queries(key, part):
    drawn = 3.0 * jnp.clip(jax.random.normal(key, (REQUEST_COUNT, DECODE_STEPS, HQ * HEAD_WIDTH), jnp.float32), -4.0, 4.0)
    return drawn.astype(jnp.bfloat16)


def draw_kept(key, part):
    request_row_keys = jax.random.split(key, REQUEST_COUNT * KEY_VALUE_HEADS)
    chosen_index = jax.vmap(lambda row_key: jax.random.permutation(row_key, HISTORY_LENGTH)[:KEPT_TOKENS])(request_row_keys)
    return chosen_index.reshape(REQUEST_COUNT, KEY_VALUE_HEADS, KEPT_TOKENS).astype(jnp.int32)


def shard_levels(stream_key, dims, shards, least, top_value):
    level = 1.0
    for axis_at, shards_of in shards:
        draws = jax.random.uniform(jax.random.fold_in(jax.random.fold_in(stream_key, 6), axis_at), (shards_of,), jnp.float32, least / len(shards), top_value / len(shards))
        level = level * jnp.repeat(jnp.exp(draws), dims[axis_at] // shards_of).reshape((-1,) + (1,) * (len(dims) - 1 - axis_at))
    return level


def shared_out(rng, own, number, rows, number_of, top, limit, slope):
    order = jax.random.permutation(rng, number_of)
    heavy_load, usual = portions_of(number_of, rows * top, limit, slope, True), portions_of(number_of, rows * top, limit, slope, False)
    places = jnp.arange(number_of)

    def named(sizes, turn):
        used = int((sizes > 0).sum())
        fixed = max(1, used // 4)
        passed = fixed + (places - fixed + turn * (used - fixed)) % max(1, number_of - fixed)
        return jnp.zeros((number_of,), jnp.int32).at[order[jnp.where(places < fixed, places, passed)]].set(jnp.asarray(sizes, jnp.int32))

    sizes = jnp.where(number % 4 == 0, named(heavy_load, number // 4), named(usual, number - number // 4 - 1))
    mixed = jax.random.permutation(jax.random.fold_in(own, 3), number_of)
    donor, taker = mixed[0:number_of // 2 * 2:2], mixed[1:number_of // 2 * 2:2]
    margin = jnp.minimum(sizes[donor] - 1, limit - sizes[taker]) // 2
    margin = jnp.where((donor == order[0]) | (taker == order[0]) | (sizes[taker] == 0), 0, jnp.maximum(margin, 0))
    passed = jax.random.randint(jax.random.fold_in(own, 4), (number_of // 2,), 0, 1 << 20) % (margin + 1)
    sizes = sizes.at[donor].add(-passed).at[taker].add(passed)
    members = jnp.searchsorted(jnp.cumsum(sizes), jnp.arange(rows * top), side="right").astype(jnp.int32)
    listing = members.reshape(top, rows).T
    listing = listing[jax.random.permutation(jax.random.fold_in(own, 1), rows)]
    turn = jax.random.randint(jax.random.fold_in(own, 2), (rows, 1), 0, top)
    return jnp.take_along_axis(listing, (jnp.arange(top)[None, :] + turn) % top, axis=1)


def portions_of(count, total, bound, lean, full):
    loads = [(1 << 20) // math.isqrt(grade ** lean) + 1 for grade in range(1, count + 1)]
    largest = bound if full else min(bound, max(-(-total // count), total * loads[0] // sum(loads)))
    least = 1 if total - largest >= count - 1 else 0
    counts, spare = [largest] + [least] * (count - 1), total - largest - least * (count - 1)
    while spare > 0:
        movable = [i for i in range(1, count) if counts[i] < largest] or [i for i in range(1, count) if counts[i] < bound]
        mass, remaining = sum([loads[i] for i in movable]), spare
        for i in movable:
            addition = min(bound - counts[i], max(1, remaining * loads[i] // mass), spare)
            counts[i] = counts[i] + addition
            spare = spare - addition
    return np.array(counts)


def normal_values(key, shape, width, bound, cuts=(), dtype=jnp.bfloat16):
    loudness = shard_levels(key, shape, cuts, -0.22, 0.18) if cuts else 1.0
    array = jax.random.normal(key, shape, jnp.float32) * width * loudness
    return jnp.minimum(jnp.maximum(array, -bound), bound).astype(dtype)


def setup_inputs(seed: int = 0) -> dict:
    streams_of = jax.random.split(jax.random.key(seed), 11)
    queries = draw_queries(jax.random.fold_in(streams_of[10], 71), 0)
    incoming_keys = normal_values(streams_of[1], (REQUEST_COUNT, DECODE_STEPS, KEY_VALUE_HEADS * HEAD_WIDTH), 1.0, 6.0, ((0, 64), (2, 2)))
    incoming_values = normal_values(streams_of[2], (REQUEST_COUNT, DECODE_STEPS, KEY_VALUE_HEADS * HEAD_WIDTH), 1.0, 6.0, ((0, 64), (2, 2)))
    system_prefix_keys = normal_values(streams_of[3], (PROMPT_COUNT, PREFIX_LENGTH, KEY_VALUE_HEADS * HEAD_WIDTH), 1.0, 6.0, ((1, 64), (2, 2)))
    system_prefix_values = normal_values(streams_of[4], (PROMPT_COUNT, PREFIX_LENGTH, KEY_VALUE_HEADS * HEAD_WIDTH), 1.0, 6.0, ((1, 64), (2, 2)))
    request_history_keys = normal_values(streams_of[5], (REQUEST_COUNT, HISTORY_LENGTH, KEY_VALUE_HEADS * HEAD_WIDTH), 1.0, 6.0, ((0, 64), (2, 2)))
    request_history_values = normal_values(streams_of[6], (REQUEST_COUNT, HISTORY_LENGTH, KEY_VALUE_HEADS * HEAD_WIDTH), 1.0, 6.0, ((0, 64), (2, 2)))
    kept = draw_kept(jax.random.fold_in(streams_of[10], 71), 0)
    membership_keys = jax.random.split(jax.random.fold_in(streams_of[8], 1), REQUEST_COUNT // REQUEST_COUNT)
    membership_turns = jax.random.permutation(jax.random.fold_in(streams_of[8], 3), REQUEST_COUNT // REQUEST_COUNT)
    membership = jax.vmap(lambda own, number: shared_out(jax.random.fold_in(streams_of[8], 2), own, number, REQUEST_COUNT, PROMPT_COUNT, 1, CAP, 2))(membership_keys, membership_turns).reshape((REQUEST_COUNT, 1))
    out_weight = normal_values(streams_of[9], (HQ * HEAD_WIDTH, D), (HQ * HEAD_WIDTH) ** -0.5, 0.0625, ((0, 2), (1, 64)))
    return dict(queries=queries, incoming_keys=incoming_keys, incoming_values=incoming_values, system_prefix_keys=system_prefix_keys, system_prefix_values=system_prefix_values, request_history_keys=request_history_keys, request_history_values=request_history_values, kept=kept, membership=membership, out_weight=out_weight)


def partial_block_result(grouped_query_heads, block_keys, block_values, allowed):
    scores = jnp.einsum('tkgd,lkd->tkgl', grouped_query_heads, block_keys.astype(jnp.float32)) * (HEAD_WIDTH ** -0.5)
    if allowed is not None:
        scores = jnp.where(allowed, scores, -1e30)
    row_peak = jnp.max(scores, axis=-1)
    exp_terms = jnp.exp(scores - row_peak[..., None])
    row_total = jnp.sum(exp_terms, axis=-1)
    rounded = lax.optimization_barrier(exp_terms.astype(jnp.bfloat16)).astype(jnp.float32)
    block_out = jnp.einsum('tkgl,lkd->tkgd', rounded, block_values.astype(jnp.float32))
    return row_peak, row_total, block_out


def one_request(items, system_prefix_keys, system_prefix_values):
    single_query_row, recent_token_keys, recent_token_values, history_key_rows, history_value_rows, retained_row, membership_row = items
    grouped_query_heads = single_query_row.astype(jnp.float32).reshape(DECODE_STEPS, KEY_VALUE_HEADS, HEADS_PER_GROUP, HEAD_WIDTH)
    system_prompt_keys = lax.dynamic_index_in_dim(system_prefix_keys, membership_row[0], 0, keepdims=False).reshape(N_REQ, PROMPT_PORTION, KEY_VALUE_HEADS, HEAD_WIDTH)
    system_prompt_values = lax.dynamic_index_in_dim(system_prefix_values, membership_row[0], 0, keepdims=False).reshape(N_REQ, PROMPT_PORTION, KEY_VALUE_HEADS, HEAD_WIDTH)
    src_peak, src_total, src_out = jax.vmap(partial_block_result, in_axes=(None, 0, 0, None))(grouped_query_heads, system_prompt_keys, system_prompt_values, None)
    head_index_list = jnp.arange(KEY_VALUE_HEADS)[None, :]
    retained_keys = history_key_rows.reshape(HISTORY_LENGTH, KEY_VALUE_HEADS, HEAD_WIDTH)[retained_row.T, head_index_list]
    retained_values = history_value_rows.reshape(HISTORY_LENGTH, KEY_VALUE_HEADS, HEAD_WIDTH)[retained_row.T, head_index_list]
    kept_peak, kept_total, kept_out = partial_block_result(grouped_query_heads, retained_keys, retained_values, None)
    causal_mask = jnp.arange(DECODE_STEPS)[None, :] <= jnp.arange(DECODE_STEPS)[:, None]
    recent_score_peak, recent_weight_sum, recent_output = partial_block_result(grouped_query_heads, recent_token_keys.reshape(DECODE_STEPS, KEY_VALUE_HEADS, HEAD_WIDTH), recent_token_values.reshape(DECODE_STEPS, KEY_VALUE_HEADS, HEAD_WIDTH), causal_mask[:, None, None, :])
    top_score = jnp.maximum(jnp.maximum(jnp.max(src_peak, axis=0), kept_peak), recent_score_peak)
    src_factor = jnp.exp(src_peak - top_score[None])
    kept_factor = jnp.exp(kept_peak - top_score)
    fresh_factor = jnp.exp(recent_score_peak - top_score)
    numerator = jnp.sum(src_factor[..., None] * src_out, axis=0) + kept_factor[..., None] * kept_out + fresh_factor[..., None] * recent_output
    denominator = jnp.sum(src_factor * src_total, axis=0) + kept_factor * kept_total + fresh_factor * recent_weight_sum
    attention = (numerator / denominator[..., None]).astype(jnp.bfloat16)
    return attention.reshape(DECODE_STEPS, HQ * HEAD_WIDTH)


def reference(queries, incoming_keys, incoming_values, system_prefix_keys, system_prefix_values, request_history_keys, request_history_values, kept, membership, out_weight):
    attention = lax.map(lambda items: one_request(items, system_prefix_keys, system_prefix_values), (queries, incoming_keys, incoming_values, request_history_keys, request_history_values, kept, membership))
    projected = jnp.dot(attention.reshape(REQUEST_COUNT * DECODE_STEPS, HQ * HEAD_WIDTH), out_weight, preferred_element_type=jnp.float32)
    return projected.astype(jnp.bfloat16).reshape(REQUEST_COUNT, DECODE_STEPS, D)
```

```python
import functools

import jax
import jax.numpy as jnp
from jax import lax
from jax.experimental import pallas as pl
from jax.experimental.pallas import tpu as pltpu
from jax.sharding import PartitionSpec as P

HEAD = 128
PROMPTS = 8
STEPS = 4
ROWS = 32
REQS = 64
CHIPS = 32
PORTION = 256
HISTORY = 2048
KEPT = 1024
PAY = 136
LOG2E = 1.4426950408889634
C2 = HEAD ** -0.5 * LOG2E
NEG = -1e30
BF = jnp.bfloat16
F32 = jnp.float32

SAME_CORE = [[2 * i + c for i in range(CHIPS)] for c in range(2)]
CORE_SWAP = [(i, i ^ 1) for i in range(REQS)]

VM = pl.BlockSpec(memory_space=pltpu.VMEM)
SM = pl.BlockSpec(memory_space=pltpu.SMEM)
HB = pl.BlockSpec(memory_space=pl.ANY)


def nt(a, b):
    return lax.dot_general(a, b, (((1,), (1,)), ((), ())), preferred_element_type=F32)


def mm(a, b):
    return lax.dot_general(a, b, (((1,), (0,)), ((), ())), preferred_element_type=F32)


def iota(shape, dim):
    return lax.broadcasted_iota(jnp.int32, shape, dim)


def pack_kernel(mem_ref, q_ref, out_ref, tmp):
    for head in range(32):
        tmp[pl.ds(head * STEPS, STEPS), :] = q_ref[0, :, pl.ds(head * HEAD, HEAD)].astype(F32)
    data = tmp[...].astype(BF)
    side = jnp.full((8, HEAD), mem_ref[0, 0], jnp.int32).astype(F32).astype(BF)
    for i in range(CHIPS):
        out_ref[i, pl.ds(0, 128), :] = data
        out_ref[i, pl.ds(128, 8), :] = side


def pack(membership, queries):
    return pl.pallas_call(
        pack_kernel,
        out_shape=jax.ShapeDtypeStruct((CHIPS, PAY, HEAD), BF),
        in_specs=[SM, VM],
        out_specs=VM,
        scratch_shapes=[pltpu.VMEM((128, HEAD), F32)],
        name="pack",
    )(membership, queries)


def private_kernel(q_ref, kept_ref, hk_ref, hv_ref, nk_ref, nv_ref, o_ref, l_ref, knew, vnew):
    ones = jnp.ones((HISTORY, HEAD), BF)
    ones_new = jnp.ones((128, HEAD), BF)
    sub_hi = iota((16, KEPT), 0)
    sub_lo = iota((128, KEPT), 0)
    col = iota((ROWS, 128), 1)
    step_of = iota((ROWS, 128), 0) & (STEPS - 1)
    new_ok = (col < STEPS) & (col <= step_of)
    knew[...] = jnp.zeros_like(knew)
    vnew[...] = jnp.zeros_like(vnew)
    for g in range(4):
        lanes = pl.ds(g * HEAD, HEAD)
        pos = kept_ref[0, pl.ds(g, 1), :]
        hot_hi = jnp.where(sub_hi == lax.shift_right_logical(pos, 7), 1.0, 0.0).astype(BF)
        hot_lo = jnp.where(sub_lo == (pos & 127), 1.0, 0.0).astype(BF)
        count = nt(hot_hi, hot_lo)
        q = q_ref[0, pl.ds(g * ROWS, ROWS), :]
        s = nt(q, hk_ref[0, :, lanes])
        s = jnp.concatenate(
            [
                jnp.where(count[i : i + 1, :] > 0.5, s[:, i * 128 : (i + 1) * 128], NEG)
                for i in range(16)
            ],
            axis=1,
        )
        knew[pl.ds(0, STEPS), :] = nk_ref[0, :, lanes].astype(F32)
        vnew[pl.ds(0, STEPS), :] = nv_ref[0, :, lanes].astype(F32)
        sn = jnp.where(new_ok, nt(q, knew[...].astype(BF)), NEG)
        peak = jnp.maximum(jnp.max(s, axis=1, keepdims=True), jnp.max(sn, axis=1, keepdims=True))
        p = jnp.exp2((s - peak) * C2).astype(BF)
        pn = jnp.exp2((sn - peak) * C2).astype(BF)
        ov = mm(p, jnp.concatenate([hv_ref[0, :, lanes], ones], axis=1))
        ov += mm(pn, jnp.concatenate([vnew[...].astype(BF), ones_new], axis=1))
        total = ov[:, HEAD:]
        o_ref[g] = ov[:, :HEAD] / total
        l_ref[g] = peak * C2 + jnp.log(total) * LOG2E


def private(packed, kept, hk, hv, nk, nv):
    return pl.pallas_call(
        private_kernel,
        out_shape=[jax.ShapeDtypeStruct((4, ROWS, HEAD), F32)] * 2,
        in_specs=[VM] * 6,
        out_specs=[VM] * 2,
        scratch_shapes=[pltpu.VMEM((128, HEAD), F32)] * 2,
        cost_estimate=pl.CostEstimate(
            flops=400_000_000, transcendentals=300_000, bytes_accessed=5_000_000
        ),
        name="private",
    )(packed[:1], kept, hk, hv, nk, nv)


def prefix_kernel(
    keep, qa_hbm, qb_hbm, k_hbm, v_hbm, po_ref, pl_ref, o_ref, l_ref,
    q, kbuf, vbuf, obuf, lbuf, tab_v, tab_s, qsem, ksem, tsem,
):
    me = lax.axis_index("req")
    core = me & 1
    pair = core if keep else 1 - core
    ca = pltpu.make_async_copy(qa_hbm, q.at[pl.ds(0, CHIPS)], qsem.at[0])
    cb = pltpu.make_async_copy(qb_hbm, q.at[pl.ds(CHIPS, CHIPS)], qsem.at[1])
    ca.start()
    cb.start()
    lanes = pl.ds(pl.multiple_of(pair * 256, 256), 256)

    def fetch(p):
        return (
            pltpu.make_async_copy(k_hbm.at[p, :, lanes], kbuf.at[p], ksem.at[p, 0]),
            pltpu.make_async_copy(v_hbm.at[p, :, lanes], vbuf.at[p], ksem.at[p, 1]),
        )

    for p in range(PROMPTS):
        for copy in fetch(p):
            copy.start()
    ca.wait()
    cb.wait()

    sides = q[:, pl.ds(128, 8), :].astype(F32)
    member = jnp.max(sides, axis=1)
    member = jnp.concatenate([member, jnp.full((64, HEAD), 99.0, F32)], axis=0)
    across = member.T
    row, lane = iota((128, 128), 0), iota((128, 128), 1)
    before = (across < member) | ((across == member) & (lane < row))
    slot = jnp.sum(jnp.where(before, 1.0, 0.0), axis=1, keepdims=True)
    here = slot == lane.astype(F32)
    rowf = row.astype(F32)
    coref = core.astype(F32)
    req = jnp.where(row < CHIPS, 2.0 * rowf + coref, 2.0 * (rowf - CHIPS) + 1.0 - coref)
    lanef = lane.astype(F32)

    def total(x):
        return jnp.sum(x, axis=0, keepdims=True)

    order = total(jnp.where(here & (row < REQS), rowf, 0.0))
    target = total(jnp.where(here, jnp.where(row < REQS, req, float(REQS)), 0.0))
    starts = total(jnp.where(member < lanef, 1.0, 0.0))
    counts = total(jnp.where(member == lanef, 1.0, 0.0))
    table = jnp.concatenate([order, target, starts, counts, jnp.zeros((4, 128), F32)], axis=0)
    tab_v[...] = table.astype(jnp.int32)
    ct = pltpu.make_async_copy(tab_v, tab_s, tsem)
    ct.start()
    ct.wait()

    ones = jnp.ones((PORTION, HEAD), BF)
    qrow = pl.multiple_of(pair * 64, 64)

    for p in range(PROMPTS):
        for copy in fetch(p):
            copy.wait()
        start = tab_s[2, p]
        chunks = lax.shift_right_logical(tab_s[3, p] + 7, 3)

        def chunk(i, carry):
            slot0 = start + i * 8
            for head in range(2):
                rows = pl.ds(qrow + head * ROWS, ROWS)
                qs = jnp.concatenate([q[tab_s[0, slot0 + j], rows, :] for j in range(8)], axis=0)
                s = nt(qs, kbuf[p, :, pl.ds(head * HEAD, HEAD)])
                peak = jnp.max(s, axis=1, keepdims=True)
                w = jnp.exp2((s - peak) * C2).astype(BF)
                ov = mm(w, jnp.concatenate([vbuf[p, :, pl.ds(head * HEAD, HEAD)], ones], axis=1))
                l = ov[:, HEAD:]
                o = ov[:, :HEAD] / l
                lse = peak * C2 + jnp.log(l) * LOG2E
                for j in range(8):
                    t = tab_s[1, slot0 + j]
                    obuf[head, t] = o[j * ROWS : (j + 1) * ROWS]
                    lbuf[head, t] = lse[j * ROWS : (j + 1) * ROWS]
            return carry

        lax.fori_loop(0, chunks, chunk, 0)

    for head in range(2):
        o1, l1 = obuf[head, me], lbuf[head, me]
        o2, l2 = po_ref[pair * 2 + head], pl_ref[pair * 2 + head]
        top = jnp.maximum(l1, l2)
        e1, e2 = jnp.exp2(l1 - top), jnp.exp2(l2 - top)
        both = e1 + e2
        obuf[head, me] = (e1 * o1 + e2 * o2) / both
        lbuf[head, me] = top + jnp.log(both) * LOG2E

    diag = row == lane
    for head in range(2):
        for grp in range(16):
            n = head * 16 + grp
            lb = lbuf[head, pl.ds(grp * 4, 4)].reshape(128, HEAD)
            l_ref[pl.ds(n, 1), :] = total(jnp.where(diag, lb, 0.0))
            ob = obuf[head, pl.ds(grp * 4, 4)].reshape(128, HEAD)
            o_ref[n] = ob.astype(o_ref.dtype)


def prefix(keep, qa, qb, k, v, po, pll):
    return pl.pallas_call(
        functools.partial(prefix_kernel, keep),
        out_shape=[
            jax.ShapeDtypeStruct((32, 128, HEAD), F32 if keep else BF),
            jax.ShapeDtypeStruct((32, 128), F32),
        ],
        in_specs=[HB, HB, HB, HB, VM, VM],
        out_specs=[VM, VM],
        scratch_shapes=[
            pltpu.VMEM((REQS, PAY, HEAD), BF),
            pltpu.VMEM((PROMPTS, PORTION, 256), BF),
            pltpu.VMEM((PROMPTS, PORTION, 256), BF),
            pltpu.VMEM((2, REQS + 1, ROWS, HEAD), F32),
            pltpu.VMEM((2, REQS + 1, ROWS, HEAD), F32),
            pltpu.VMEM((8, 128), jnp.int32),
            pltpu.SMEM((8, 128), jnp.int32),
            pltpu.SemaphoreType.DMA((2,)),
            pltpu.SemaphoreType.DMA((PROMPTS, 2)),
            pltpu.SemaphoreType.DMA(()),
        ],
        cost_estimate=pl.CostEstimate(
            flops=600_000_000, transcendentals=1_000_000, bytes_accessed=6_000_000
        ),
        name="prefix_keep" if keep else "prefix_send",
    )(qa, qb, k, v, po, pll)


def merge_kernel(o1_ref, l1_ref, o2_ref, l2_ref, out_ref):
    l1, l2 = l1_ref[...], l2_ref[...]
    top = jnp.maximum(l1, l2)
    e1, e2 = jnp.exp2(l1 - top), jnp.exp2(l2 - top)
    both = e1 + e2
    w1 = e1 / both
    lse = top + jnp.log(both) * LOG2E
    hi = lse.astype(BF).astype(F32)
    mid = (lse - hi).astype(BF).astype(F32)
    lo = lse - hi - mid
    cols = jnp.concatenate([w1, jnp.zeros((96, 128), F32)], axis=0).T
    sub = iota((8, 128), 0)
    for n in range(32):
        w = cols[:, n : n + 1]
        o2 = o2_ref[n].astype(F32)
        out_ref[n, pl.ds(0, 128), :] = (o2 + w * (o1_ref[n] - o2)).astype(BF)
        side = jnp.where(
            sub == 0, hi[n : n + 1], jnp.where(sub == 1, mid[n : n + 1], jnp.where(sub == 2, lo[n : n + 1], 0.0))
        )
        out_ref[n, pl.ds(128, 8), :] = side.astype(BF)


def merge(o1, l1, o2, l2):
    return pl.pallas_call(
        merge_kernel,
        out_shape=jax.ShapeDtypeStruct((CHIPS, PAY, HEAD), BF),
        in_specs=[VM] * 4,
        out_specs=VM,
        name="merge",
    )(o1, l1, o2, l2)


def combine_kernel(in_ref, out_ref, acc_ref):
    pieces = [in_ref[n, pl.ds(128, 8), :].astype(F32) for n in range(CHIPS)]
    lse = jnp.concatenate([x[0:1] + x[1:2] + x[2:3] for x in pieces], axis=0)
    top = jnp.max(lse, axis=0, keepdims=True)
    e = jnp.exp2(lse - top)
    w = e / jnp.sum(e, axis=0, keepdims=True)
    cols = jnp.concatenate([w, jnp.zeros((96, 128), F32)], axis=0).T
    acc = jnp.zeros((128, HEAD), F32)
    for n in range(CHIPS):
        acc += cols[:, n : n + 1] * in_ref[n, pl.ds(0, 128), :].astype(F32)
    for r in range(4):
        for h in range(8):
            at = r * ROWS + h * STEPS
            acc_ref[pl.ds(h * 16 + r * STEPS, STEPS), :] = acc[at : at + STEPS]
    att = acc_ref[...].astype(BF)
    for n in range(CHIPS):
        out_ref[n] = att


def combine(x):
    return pl.pallas_call(
        combine_kernel,
        out_shape=jax.ShapeDtypeStruct((CHIPS, 128, HEAD), BF),
        in_specs=[VM],
        out_specs=VM,
        scratch_shapes=[pltpu.VMEM((128, HEAD), F32)],
        name="combine",
    )(x)


def project_kernel(own, *refs):
    if own:
        a_ref, w_hbm, out_ref, w, sem = refs
        acc = jnp.zeros((REQS * STEPS, 128), F32)
    else:
        a_ref, w_hbm, base_ref, out_ref, w, sem = refs
        acc = base_ref[...]
    core = lax.axis_index("req") & 1
    pair = core if own else 1 - core
    copy = pltpu.make_async_copy(w_hbm.at[pl.ds(pl.multiple_of(pair * 2048, 2048), 2048), :], w, sem)
    copy.start()
    copy.wait()
    for z in range(2):
        for h in range(0, 8, 2):
            a = jnp.concatenate(
                [
                    a_ref[pl.ds(z * 16, 16), pl.ds((h + i) * 16, 16), :].reshape(256, HEAD)
                    for i in range(2)
                ],
                axis=1,
            )
            acc += mm(a, w[pl.ds((z * 8 + h) * 128, 256), :])
    out_ref[...] = acc


def project(own, a, w, *base):
    return pl.pallas_call(
        functools.partial(project_kernel, own),
        out_shape=jax.ShapeDtypeStruct((REQS * STEPS, 128), F32),
        in_specs=[VM, HB] + [VM] * len(base),
        out_specs=VM,
        scratch_shapes=[pltpu.VMEM((2048, 128), BF), pltpu.SemaphoreType.DMA(())],
        cost_estimate=pl.CostEstimate(
            flops=140_000_000, transcendentals=0, bytes_accessed=2_000_000
        ),
        name="project_own" if own else "project_other",
    )(a, w, *base)


def over_chips(x):
    return lax.all_to_all(
        x, "req", split_axis=0, concat_axis=0, axis_index_groups=SAME_CORE, tiled=True
    )


def swap_cores(x):
    return lax.ppermute(x, "req", CORE_SWAP)


def local(queries, nk, nv, pk, pv, hk, hv, kept, membership, out_weight):
    packed = pack(membership, queries)
    qa = over_chips(packed)
    qb = swap_cores(qa)
    po, pll = private(packed, kept, hk, hv, nk, nv)
    send_o, send_l = prefix(False, qa, qb, pk, pv, po, pll)
    got_o, got_l = swap_cores(send_o), swap_cores(send_l)
    keep_o, keep_l = prefix(True, qa, qb, pk, pv, po, pll)
    parts = over_chips(merge(keep_o, keep_l, got_o, got_l))
    att = over_chips(combine(parts))
    att_other = swap_cores(att)
    half = project(True, att, out_weight)
    mine = project(False, att_other, out_weight, half)
    theirs = lax.ppermute(mine, "kvh", [(0, 1), (1, 0)])
    return (mine + theirs).astype(BF).reshape(REQS, STEPS, 128)


def solution(mesh):
    placed = (
        P("req", None, "kvh"),
        P("req", None, "kvh"),
        P("req", None, "kvh"),
        P(None, "req", "kvh"),
        P(None, "req", "kvh"),
        P("req", None, "kvh"),
        P("req", None, "kvh"),
        P("req", "kvh", None),
        P("req", None),
        P("kvh", "req"),
    )
    return jax.shard_map(
        local, mesh=mesh, in_specs=placed, out_specs=P(None, None, "req"), check_vma=False
    )
```

```python
import functools

import jax
import jax.numpy as jnp
from jax import lax
from jax.experimental import pallas as pl
from jax.experimental.pallas import tpu as pltpu
from jax.sharding import PartitionSpec as P

HEAD = 128
PROMPTS = 8
STEPS = 4
ROWS = 32
REQS = 64
CHIPS = 32
PORTION = 256
HISTORY = 2048
KEPT = 1024
PAY = 136
LOG2E = 1.4426950408889634
C2 = HEAD ** -0.5 * LOG2E
NEG = -1e30
BF = jnp.bfloat16
F32 = jnp.float32

SAME_CORE = [[2 * i + c for i in range(CHIPS)] for c in range(2)]
CORE_SWAP = [(i, i ^ 1) for i in range(REQS)]

LIMIT = pltpu.CompilerParams(vmem_limit_bytes=24 << 20)

VM = pl.BlockSpec(memory_space=pltpu.VMEM)
SM = pl.BlockSpec(memory_space=pltpu.SMEM)
HB = pl.BlockSpec(memory_space=pl.ANY)


def nt(a, b):
    return lax.dot_general(a, b, (((1,), (1,)), ((), ())), preferred_element_type=F32)


def mm(a, b):
    return lax.dot_general(a, b, (((1,), (0,)), ((), ())), preferred_element_type=F32)


def iota(shape, dim):
    return lax.broadcasted_iota(jnp.int32, shape, dim)


def pack_kernel(mem_ref, q_ref, out_ref, own_ref, tmp):
    for head in range(32):
        tmp[pl.ds(head * STEPS, STEPS), :] = q_ref[0, :, pl.ds(head * HEAD, HEAD)].astype(F32)
    data = tmp[...].astype(BF)
    own_ref[...] = data
    side = jnp.full((8, HEAD), mem_ref[0, 0], jnp.int32).astype(F32).astype(BF)
    for i in range(CHIPS):
        out_ref[i, pl.ds(0, 128), :] = data
        out_ref[i, pl.ds(128, 8), :] = side


def pack(membership, queries):
    return pl.pallas_call(
        pack_kernel,
        out_shape=[
            jax.ShapeDtypeStruct((CHIPS, PAY, HEAD), BF),
            jax.ShapeDtypeStruct((128, HEAD), BF),
        ],
        in_specs=[SM, VM],
        out_specs=[VM, VM],
        scratch_shapes=[pltpu.VMEM((128, HEAD), F32)],
        compiler_params=LIMIT,
        name="pack",
    )(membership, queries)


def private_kernel(q_ref, kept_ref, hk_ref, hv_ref, nk_ref, nv_ref, o_ref, l_ref, knew, vnew):
    ones = jnp.ones((HISTORY, HEAD), BF)
    ones_new = jnp.ones((128, HEAD), BF)
    sub_hi = iota((16, KEPT), 0)
    sub_lo = iota((128, KEPT), 0)
    col = iota((ROWS, 128), 1)
    step_of = iota((ROWS, 128), 0) & (STEPS - 1)
    new_ok = (col < STEPS) & (col <= step_of)
    knew[...] = jnp.zeros_like(knew)
    vnew[...] = jnp.zeros_like(vnew)
    for g in range(4):
        lanes = pl.ds(g * HEAD, HEAD)
        pos = kept_ref[0, pl.ds(g, 1), :]
        hot_hi = jnp.where(sub_hi == lax.shift_right_logical(pos, 7), 1.0, 0.0).astype(BF)
        hot_lo = jnp.where(sub_lo == (pos & 127), 1.0, 0.0).astype(BF)
        count = nt(hot_hi, hot_lo)
        q = q_ref[pl.ds(g * ROWS, ROWS), :]
        s = nt(q, hk_ref[0, :, lanes])
        s = jnp.concatenate(
            [
                jnp.where(count[i : i + 1, :] > 0.5, s[:, i * 128 : (i + 1) * 128], NEG)
                for i in range(16)
            ],
            axis=1,
        )
        knew[pl.ds(0, STEPS), :] = nk_ref[0, :, lanes].astype(F32)
        vnew[pl.ds(0, STEPS), :] = nv_ref[0, :, lanes].astype(F32)
        sn = jnp.where(new_ok, nt(q, knew[...].astype(BF)), NEG)
        peak = jnp.maximum(jnp.max(s, axis=1, keepdims=True), jnp.max(sn, axis=1, keepdims=True))
        p = jnp.exp2((s - peak) * C2).astype(BF)
        pn = jnp.exp2((sn - peak) * C2).astype(BF)
        ov = mm(p, jnp.concatenate([hv_ref[0, :, lanes], ones], axis=1))
        ov += mm(pn, jnp.concatenate([vnew[...].astype(BF), ones_new], axis=1))
        total = ov[:, HEAD:]
        o_ref[g] = ov[:, :HEAD] / total
        l_ref[g] = peak * C2 + jnp.log(total) * LOG2E


def private(own, kept, hk, hv, nk, nv):
    return pl.pallas_call(
        private_kernel,
        out_shape=[jax.ShapeDtypeStruct((4, ROWS, HEAD), F32)] * 2,
        in_specs=[VM] * 6,
        out_specs=[VM] * 2,
        scratch_shapes=[pltpu.VMEM((128, HEAD), F32)] * 2,
        cost_estimate=pl.CostEstimate(
            flops=400_000_000, transcendentals=300_000, bytes_accessed=5_000_000
        ),
        compiler_params=LIMIT,
        name="private",
    )(own, kept, hk, hv, nk, nv)


def prefix_kernel(
    keep, qa_hbm, qb_hbm, k_hbm, v_hbm, po_ref, pl_ref, o_ref, l_ref,
    q, kbuf, vbuf, obuf, lbuf, tab_v, tab_s, qsem, ksem, tsem,
):
    me = lax.axis_index("req")
    core = me & 1
    pair = core if keep else 1 - core
    ca = pltpu.make_async_copy(qa_hbm, q.at[pl.ds(0, CHIPS)], qsem.at[0])
    cb = pltpu.make_async_copy(qb_hbm, q.at[pl.ds(CHIPS, CHIPS)], qsem.at[1])
    ca.start()
    cb.start()
    lanes = pl.ds(pl.multiple_of(pair * 256, 256), 256)

    def fetch(p):
        return (
            pltpu.make_async_copy(k_hbm.at[p, :, lanes], kbuf.at[p], ksem.at[p, 0]),
            pltpu.make_async_copy(v_hbm.at[p, :, lanes], vbuf.at[p], ksem.at[p, 1]),
        )

    for p in range(PROMPTS):
        for copy in fetch(p):
            copy.start()
    ca.wait()
    cb.wait()

    sides = q[:, pl.ds(128, 8), :].astype(F32)
    member = jnp.max(sides, axis=1)
    member = jnp.concatenate([member, jnp.full((64, HEAD), 99.0, F32)], axis=0)
    across = member.T
    row, lane = iota((128, 128), 0), iota((128, 128), 1)
    before = (across < member) | ((across == member) & (lane < row))
    slot = jnp.sum(jnp.where(before, 1.0, 0.0), axis=1, keepdims=True)
    here = slot == lane.astype(F32)
    rowf = row.astype(F32)
    coref = core.astype(F32)
    req = jnp.where(row < CHIPS, 2.0 * rowf + coref, 2.0 * (rowf - CHIPS) + 1.0 - coref)
    lanef = lane.astype(F32)

    def total(x):
        return jnp.sum(x, axis=0, keepdims=True)

    order = total(jnp.where(here & (row < REQS), rowf, 0.0))
    target = total(jnp.where(here, jnp.where(row < REQS, req, float(REQS)), 0.0))
    starts = total(jnp.where(member < lanef, 1.0, 0.0))
    counts = total(jnp.where(member == lanef, 1.0, 0.0))
    table = jnp.concatenate([order, target, starts, counts, jnp.zeros((4, 128), F32)], axis=0)
    tab_v[...] = table.astype(jnp.int32)
    ct = pltpu.make_async_copy(tab_v, tab_s, tsem)
    ct.start()
    ct.wait()

    ones = jnp.ones((PORTION, HEAD), BF)
    qrow = pl.multiple_of(pair * 64, 64)

    for p in range(PROMPTS):
        for copy in fetch(p):
            copy.wait()
        start = tab_s[2, p]
        chunks = lax.shift_right_logical(tab_s[3, p] + 7, 3)

        def chunk(i, carry):
            slot0 = start + i * 8
            for head in range(2):
                rows = pl.ds(qrow + head * ROWS, ROWS)
                qs = jnp.concatenate([q[tab_s[0, slot0 + j], rows, :] for j in range(8)], axis=0)
                s = nt(qs, kbuf[p, :, pl.ds(head * HEAD, HEAD)])
                peak = jnp.max(s, axis=1, keepdims=True)
                w = jnp.exp2((s - peak) * C2).astype(BF)
                ov = mm(w, jnp.concatenate([vbuf[p, :, pl.ds(head * HEAD, HEAD)], ones], axis=1))
                l = ov[:, HEAD:]
                o = ov[:, :HEAD] / l
                lse = peak * C2 + jnp.log(l) * LOG2E
                for j in range(8):
                    t = tab_s[1, slot0 + j]
                    obuf[head, t] = o[j * ROWS : (j + 1) * ROWS]
                    lbuf[head, t] = lse[j * ROWS : (j + 1) * ROWS]
            return carry

        lax.fori_loop(0, chunks, chunk, 0)

    for head in range(2):
        o1, l1 = obuf[head, me], lbuf[head, me]
        o2, l2 = po_ref[pair * 2 + head], pl_ref[pair * 2 + head]
        top = jnp.maximum(l1, l2)
        e1, e2 = jnp.exp2(l1 - top), jnp.exp2(l2 - top)
        both = e1 + e2
        obuf[head, me] = (e1 * o1 + e2 * o2) / both
        lbuf[head, me] = top + jnp.log(both) * LOG2E

    diag = row == lane
    for head in range(2):
        for grp in range(16):
            n = head * 16 + grp
            lb = lbuf[head, pl.ds(grp * 4, 4)].reshape(128, HEAD)
            l_ref[pl.ds(n, 1), :] = total(jnp.where(diag, lb, 0.0))
            ob = obuf[head, pl.ds(grp * 4, 4)].reshape(128, HEAD)
            o_ref[n] = ob.astype(o_ref.dtype)


def prefix(keep, qa, qb, k, v, po, pll):
    return pl.pallas_call(
        functools.partial(prefix_kernel, keep),
        out_shape=[
            jax.ShapeDtypeStruct((32, 128, HEAD), F32 if keep else BF),
            jax.ShapeDtypeStruct((32, 128), F32),
        ],
        in_specs=[HB, HB, HB, HB, VM, VM],
        out_specs=[VM, VM],
        scratch_shapes=[
            pltpu.VMEM((REQS, PAY, HEAD), BF),
            pltpu.VMEM((PROMPTS, PORTION, 256), BF),
            pltpu.VMEM((PROMPTS, PORTION, 256), BF),
            pltpu.VMEM((2, REQS + 1, ROWS, HEAD), F32),
            pltpu.VMEM((2, REQS + 1, ROWS, HEAD), F32),
            pltpu.VMEM((8, 128), jnp.int32),
            pltpu.SMEM((8, 128), jnp.int32),
            pltpu.SemaphoreType.DMA((2,)),
            pltpu.SemaphoreType.DMA((PROMPTS, 2)),
            pltpu.SemaphoreType.DMA(()),
        ],
        cost_estimate=pl.CostEstimate(
            flops=600_000_000, transcendentals=1_000_000, bytes_accessed=6_000_000
        ),
        compiler_params=LIMIT,
        name="prefix_keep" if keep else "prefix_send",
    )(qa, qb, k, v, po, pll)


def merge_kernel(o1_ref, l1_ref, o2_ref, l2_ref, out_ref):
    l1, l2 = l1_ref[...], l2_ref[...]
    top = jnp.maximum(l1, l2)
    e1, e2 = jnp.exp2(l1 - top), jnp.exp2(l2 - top)
    both = e1 + e2
    w1 = e1 / both
    lse = top + jnp.log(both) * LOG2E
    hi = lse.astype(BF).astype(F32)
    mid = (lse - hi).astype(BF).astype(F32)
    lo = lse - hi - mid
    cols = jnp.concatenate([w1, jnp.zeros((96, 128), F32)], axis=0).T
    sub = iota((8, 128), 0)
    for n in range(32):
        w = cols[:, n : n + 1]
        o2 = o2_ref[n].astype(F32)
        out_ref[n, pl.ds(0, 128), :] = (o2 + w * (o1_ref[n] - o2)).astype(BF)
        side = jnp.where(
            sub == 0, hi[n : n + 1], jnp.where(sub == 1, mid[n : n + 1], jnp.where(sub == 2, lo[n : n + 1], 0.0))
        )
        out_ref[n, pl.ds(128, 8), :] = side.astype(BF)


def merge(o1, l1, o2, l2):
    return pl.pallas_call(
        merge_kernel,
        out_shape=jax.ShapeDtypeStruct((CHIPS, PAY, HEAD), BF),
        in_specs=[VM] * 4,
        out_specs=VM,
        compiler_params=LIMIT,
        name="merge",
    )(o1, l1, o2, l2)


def combine_kernel(in_ref, out_ref, acc_ref):
    pieces = [in_ref[n, pl.ds(128, 8), :].astype(F32) for n in range(CHIPS)]
    lse = jnp.concatenate([x[0:1] + x[1:2] + x[2:3] for x in pieces], axis=0)
    top = jnp.max(lse, axis=0, keepdims=True)
    e = jnp.exp2(lse - top)
    w = e / jnp.sum(e, axis=0, keepdims=True)
    cols = jnp.concatenate([w, jnp.zeros((96, 128), F32)], axis=0).T
    acc = jnp.zeros((128, HEAD), F32)
    for n in range(CHIPS):
        acc += cols[:, n : n + 1] * in_ref[n, pl.ds(0, 128), :].astype(F32)
    for r in range(4):
        for h in range(8):
            at = r * ROWS + h * STEPS
            acc_ref[pl.ds(h * 16 + r * STEPS, STEPS), :] = acc[at : at + STEPS]
    att = acc_ref[...].astype(BF)
    for n in range(CHIPS):
        out_ref[n] = att


def combine(x):
    return pl.pallas_call(
        combine_kernel,
        out_shape=jax.ShapeDtypeStruct((CHIPS, 128, HEAD), BF),
        in_specs=[VM],
        out_specs=VM,
        scratch_shapes=[pltpu.VMEM((128, HEAD), F32)],
        compiler_params=LIMIT,
        name="combine",
    )(x)


def project_kernel(own, *refs):
    if own:
        a_ref, w_hbm, out_ref, w, sem = refs
        acc = jnp.zeros((REQS * STEPS, 128), F32)
    else:
        a_ref, w_hbm, base_ref, out_ref, w, sem = refs
        acc = base_ref[...]
    core = lax.axis_index("req") & 1
    pair = core if own else 1 - core
    copy = pltpu.make_async_copy(w_hbm.at[pl.ds(pl.multiple_of(pair * 2048, 2048), 2048), :], w, sem)
    copy.start()
    copy.wait()
    for z in range(2):
        for h in range(0, 8, 2):
            a = jnp.concatenate(
                [
                    a_ref[pl.ds(z * 16, 16), pl.ds((h + i) * 16, 16), :].reshape(256, HEAD)
                    for i in range(2)
                ],
                axis=1,
            )
            acc += mm(a, w[pl.ds((z * 8 + h) * 128, 256), :])
    out_ref[...] = acc


def project(own, a, w, *base):
    return pl.pallas_call(
        functools.partial(project_kernel, own),
        out_shape=jax.ShapeDtypeStruct((REQS * STEPS, 128), F32),
        in_specs=[VM, HB] + [VM] * len(base),
        out_specs=VM,
        scratch_shapes=[pltpu.VMEM((2048, 128), BF), pltpu.SemaphoreType.DMA(())],
        cost_estimate=pl.CostEstimate(
            flops=140_000_000, transcendentals=0, bytes_accessed=2_000_000
        ),
        compiler_params=LIMIT,
        name="project_own" if own else "project_other",
    )(a, w, *base)


def over_chips(x):
    return lax.all_to_all(
        x, "req", split_axis=0, concat_axis=0, axis_index_groups=SAME_CORE, tiled=True
    )


def swap_cores(x):
    return lax.ppermute(x, "req", CORE_SWAP)


def local(queries, nk, nv, pk, pv, hk, hv, kept, membership, out_weight):
    packed, own = pack(membership, queries)
    qa = over_chips(packed)
    po, pll = private(own, kept, hk, hv, nk, nv)
    qa, po, pll = lax.optimization_barrier((qa, po, pll))
    qb = swap_cores(qa)
    send_o, send_l = prefix(False, qa, qb, pk, pv, po, pll)
    got_o, got_l = swap_cores(send_o), swap_cores(send_l)
    keep_o, keep_l = prefix(True, qa, qb, pk, pv, po, pll)
    parts = over_chips(merge(keep_o, keep_l, got_o, got_l))
    att = over_chips(combine(parts))
    att_other = swap_cores(att)
    half = project(True, att, out_weight)
    mine = project(False, att_other, out_weight, half)
    theirs = lax.ppermute(mine, "kvh", [(0, 1), (1, 0)])
    return (mine + theirs).astype(BF).reshape(REQS, STEPS, 128)


def solution(mesh):
    placed = (
        P("req", None, "kvh"),
        P("req", None, "kvh"),
        P("req", None, "kvh"),
        P(None, "req", "kvh"),
        P(None, "req", "kvh"),
        P("req", None, "kvh"),
        P("req", None, "kvh"),
        P("req", "kvh", None),
        P("req", None),
        P("kvh", "req"),
    )
    return jax.shard_map(
        local, mesh=mesh, in_specs=placed, out_specs=P(None, None, "req"), check_vma=False
    )
```

```python
import jax
import jax.numpy as jnp
from jax import lax
from jax.experimental import pallas as pl
from jax.experimental.pallas import tpu as pltpu
from jax.sharding import PartitionSpec as P

HEAD = 128
PROMPTS = 8
STEPS = 4
ROWS = 32
REQS = 64
CHIPS = 32
PORTION = 256
HISTORY = 2048
KEPT = 1024
GROUP = 4
PAY = 136
LOG2E = 1.4426950408889634
C2 = HEAD ** -0.5 * LOG2E
NEG = -1e30
BF = jnp.bfloat16
F32 = jnp.float32

SAME_CORE = [[2 * i + c for i in range(CHIPS)] for c in range(2)]
CORE_SWAP = [(i, i ^ 1) for i in range(REQS)]

LIMIT = pltpu.CompilerParams(vmem_limit_bytes=24 << 20)

VM = pl.BlockSpec(memory_space=pltpu.VMEM)
SM = pl.BlockSpec(memory_space=pltpu.SMEM)
HB = pl.BlockSpec(memory_space=pltpu.HBM)


def in_hbm(x):
    return pltpu.with_memory_space_constraint(x, pltpu.HBM)


def nt(a, b):
    return lax.dot_general(a, b, (((1,), (1,)), ((), ())), preferred_element_type=F32)


def mm(a, b):
    return lax.dot_general(a, b, (((1,), (0,)), ((), ())), preferred_element_type=F32)


def iota(shape, dim):
    return lax.broadcasted_iota(jnp.int32, shape, dim)


def spread(tile, out_ref, sem):
    copies = [pltpu.make_async_copy(tile, out_ref.at[i], sem.at[i]) for i in range(CHIPS)]
    for copy in copies:
        copy.start()
    for copy in copies:
        copy.wait()


def pack_kernel(mem_ref, q_ref, out_ref, own_ref, tmp, tile, sem):
    for head in range(32):
        tmp[pl.ds(head * STEPS, STEPS), :] = q_ref[0, :, pl.ds(head * HEAD, HEAD)].astype(F32)
    data = tmp[...].astype(BF)
    own_ref[...] = data
    side = jnp.full((8, HEAD), mem_ref[0, 0], jnp.int32).astype(F32).astype(BF)
    tile[pl.ds(0, 128), :] = data
    tile[pl.ds(128, 8), :] = side
    spread(tile, out_ref, sem)


def pack(membership, queries):
    return pl.pallas_call(
        pack_kernel,
        out_shape=[
            pltpu.HBM((CHIPS, PAY, HEAD), BF),
            jax.ShapeDtypeStruct((128, HEAD), BF),
        ],
        in_specs=[SM, VM],
        out_specs=[HB, VM],
        scratch_shapes=[
            pltpu.VMEM((128, HEAD), F32),
            pltpu.VMEM((PAY, HEAD), BF),
            pltpu.SemaphoreType.DMA((CHIPS,)),
        ],
        compiler_params=LIMIT,
        name="pack",
    )(membership, queries)


def private_kernel(q_ref, kept_ref, hk_ref, hv_ref, nk_ref, nv_ref, o_ref, l_ref, knew, vnew):
    ones = jnp.ones((HISTORY, HEAD), BF)
    ones_new = jnp.ones((128, HEAD), BF)
    sub_hi = iota((16, KEPT), 0)
    sub_lo = iota((128, KEPT), 0)
    col = iota((ROWS, 128), 1)
    step_of = iota((ROWS, 128), 0) & (STEPS - 1)
    new_ok = (col < STEPS) & (col <= step_of)
    knew[...] = jnp.zeros_like(knew)
    vnew[...] = jnp.zeros_like(vnew)
    for g in range(4):
        lanes = pl.ds(g * HEAD, HEAD)
        pos = kept_ref[0, pl.ds(g, 1), :]
        hot_hi = jnp.where(sub_hi == lax.shift_right_logical(pos, 7), 1.0, 0.0).astype(BF)
        hot_lo = jnp.where(sub_lo == (pos & 127), 1.0, 0.0).astype(BF)
        count = nt(hot_hi, hot_lo)
        q = q_ref[pl.ds(g * ROWS, ROWS), :]
        s = nt(q, hk_ref[0, :, lanes])
        s = jnp.concatenate(
            [
                jnp.where(count[i : i + 1, :] > 0.5, s[:, i * 128 : (i + 1) * 128], NEG)
                for i in range(16)
            ],
            axis=1,
        )
        knew[pl.ds(0, STEPS), :] = nk_ref[0, :, lanes].astype(F32)
        vnew[pl.ds(0, STEPS), :] = nv_ref[0, :, lanes].astype(F32)
        sn = jnp.where(new_ok, nt(q, knew[...].astype(BF)), NEG)
        peak = jnp.maximum(jnp.max(s, axis=1, keepdims=True), jnp.max(sn, axis=1, keepdims=True))
        p = jnp.exp2((s - peak) * C2).astype(BF)
        pn = jnp.exp2((sn - peak) * C2).astype(BF)
        ov = mm(p, jnp.concatenate([hv_ref[0, :, lanes], ones], axis=1))
        ov += mm(pn, jnp.concatenate([vnew[...].astype(BF), ones_new], axis=1))
        total = ov[:, HEAD:]
        o_ref[g] = ov[:, :HEAD] / total
        l_ref[g] = peak * C2 + jnp.log(total) * LOG2E


def private(own, kept, hk, hv, nk, nv):
    return pl.pallas_call(
        private_kernel,
        out_shape=[jax.ShapeDtypeStruct((4, ROWS, HEAD), F32)] * 2,
        in_specs=[VM] * 6,
        out_specs=[VM] * 2,
        scratch_shapes=[pltpu.VMEM((128, HEAD), F32)] * 2,
        cost_estimate=pl.CostEstimate(
            flops=400_000_000, transcendentals=300_000, bytes_accessed=5_000_000
        ),
        compiler_params=LIMIT,
        name="private",
    )(own, kept, hk, hv, nk, nv)


def prefix_kernel(q, k0h, v0h, k1h, v1h, out_ref, k0, v0, k1, v1, lbuf, tab_v, tab_s, tsem, ksem):
    def fetch(p):
        pairs = ((k0h, k0), (v0h, v0), (k1h, k1), (v1h, v1))
        return [pltpu.make_async_copy(a.at[p], b.at[p], ksem.at[p, i]) for i, (a, b) in enumerate(pairs)]

    for p in range(PROMPTS):
        for copy in fetch(p):
            copy.start()

    sides = q[:, pl.ds(128, 8), :].astype(F32)
    member = jnp.max(sides, axis=1)
    member = jnp.concatenate([member, jnp.full((96, HEAD), 99.0, F32)], axis=0)
    across = member.T
    row, lane = iota((128, 128), 0), iota((128, 128), 1)
    before = (across < member) | ((across == member) & (lane < row))
    slot = jnp.sum(jnp.where(before, 1.0, 0.0), axis=1, keepdims=True)
    lanef = lane.astype(F32)
    here = slot == jnp.minimum(lanef, CHIPS - 1.0)

    def total(x):
        return jnp.sum(x, axis=0, keepdims=True)

    order = total(jnp.where(here, row.astype(F32), 0.0))
    starts = total(jnp.where(member < lanef, 1.0, 0.0))
    counts = total(jnp.where(member == lanef, 1.0, 0.0))
    table = jnp.concatenate([order, starts, counts, jnp.zeros((5, 128), F32)], axis=0)
    tab_v[...] = table.astype(jnp.int32)
    ct = pltpu.make_async_copy(tab_v, tab_s, tsem)
    ct.start()
    ct.wait()

    ones = jnp.ones((PORTION, HEAD), BF)

    def prompt(p, carry):
        for copy in fetch(p):
            copy.wait()
        start = tab_s[1, p]
        chunks = (tab_s[2, p] + GROUP - 1) // GROUP

        def chunk(i, c):
            slot0 = start + i * GROUP
            at = [tab_s[0, slot0 + j] for j in range(GROUP)]
            for g in range(4):
                rows, lanes = pl.ds(g * ROWS, ROWS), pl.ds(g * HEAD, HEAD)
                qs = jnp.concatenate([q[t, rows, :] for t in at], axis=0)
                s0 = nt(qs, k0[p, :, lanes])
                s1 = nt(qs, k1[p, :, lanes])
                peak = jnp.maximum(jnp.max(s0, axis=1, keepdims=True), jnp.max(s1, axis=1, keepdims=True))
                w0 = jnp.exp2((s0 - peak) * C2).astype(BF)
                w1 = jnp.exp2((s1 - peak) * C2).astype(BF)
                ov = mm(w0, jnp.concatenate([v0[p, :, lanes], ones], axis=1))
                ov += mm(w1, jnp.concatenate([v1[p, :, lanes], ones], axis=1))
                l = ov[:, HEAD:]
                o = (ov[:, :HEAD] / l).astype(BF)
                lse = peak * C2 + jnp.log(l) * LOG2E
                for j in reversed(range(GROUP)):
                    out_ref[at[j], rows, :] = o[j * ROWS : (j + 1) * ROWS]
                    lbuf[at[j], rows, :] = lse[j * ROWS : (j + 1) * ROWS]
            return c

        return lax.fori_loop(0, chunks, chunk, carry)

    lax.fori_loop(0, PROMPTS, prompt, 0)

    diag = row == lane
    sub = iota((8, 128), 0)
    for n in range(CHIPS):
        lse = total(jnp.where(diag, lbuf[n], 0.0))
        hi = lse.astype(BF).astype(F32)
        mid = (lse - hi).astype(BF).astype(F32)
        lo = lse - hi - mid
        side = jnp.where(sub == 0, hi, jnp.where(sub == 1, mid, jnp.where(sub == 2, lo, 0.0)))
        out_ref[n, pl.ds(128, 8), :] = side.astype(BF)


def prefix(q, k0, v0, k1, v1):
    return pl.pallas_call(
        prefix_kernel,
        out_shape=jax.ShapeDtypeStruct((CHIPS, PAY, HEAD), BF),
        in_specs=[VM] + [HB] * 4,
        out_specs=VM,
        scratch_shapes=[pltpu.VMEM((PROMPTS, PORTION, 512), BF)] * 4
        + [
            pltpu.VMEM((CHIPS, 128, HEAD), F32),
            pltpu.VMEM((8, 128), jnp.int32),
            pltpu.SMEM((8, 128), jnp.int32),
            pltpu.SemaphoreType.DMA(()),
            pltpu.SemaphoreType.DMA((PROMPTS, 4)),
        ],
        compiler_params=LIMIT,
        cost_estimate=pl.CostEstimate(
            flops=1_200_000_000, transcendentals=2_000_000, bytes_accessed=10_000_000
        ),
        name="prefix",
    )(q, in_hbm(k0), in_hbm(v0), k1, v1)


def combine_kernel(in_ref, po_ref, pl_ref, out_ref, tile, sem):
    row, lane = iota((128, 128), 0), iota((128, 128), 1)
    own = jnp.sum(jnp.where(row == lane, pl_ref[...].reshape(128, 128), 0.0), axis=0, keepdims=True)
    pieces = [in_ref[n, pl.ds(128, 8), :].astype(F32) for n in range(CHIPS)]
    lse = jnp.concatenate([x[0:1] + x[1:2] + x[2:3] for x in pieces], axis=0)
    top = jnp.maximum(jnp.max(lse, axis=0, keepdims=True), own)
    e, eo = jnp.exp2(lse - top), jnp.exp2(own - top)
    both = jnp.sum(e, axis=0, keepdims=True) + eo
    cols = jnp.concatenate([e / both, jnp.zeros((95, 128), F32), eo / both], axis=0).T
    acc = cols[:, 127:128] * po_ref[...].reshape(128, HEAD)
    for n in range(CHIPS):
        acc += cols[:, n : n + 1] * in_ref[n, pl.ds(0, 128), :].astype(F32)
    sub = iota((8, 128), 0)
    tiles = []
    for j in range(16):
        g, h = j // 8, j % 8
        a = acc[g * ROWS + h // 2 * 8 : g * ROWS + h // 2 * 8 + 8]
        b = acc[(g + 2) * ROWS + h // 2 * 8 : (g + 2) * ROWS + h // 2 * 8 + 8]
        if h % 2 == 0:
            tiles.append(jnp.where(sub < STEPS, a, pltpu.roll(b, STEPS, 0)))
        else:
            tiles.append(jnp.where(sub < STEPS, pltpu.roll(a, STEPS, 0), b))
    tile[...] = jnp.concatenate(tiles, axis=1).astype(BF)
    spread(tile, out_ref, sem)


def combine(x, po, pll):
    return pl.pallas_call(
        combine_kernel,
        out_shape=jax.ShapeDtypeStruct((CHIPS, 8, 2048), BF),
        in_specs=[VM] * 3,
        out_specs=HB,
        scratch_shapes=[pltpu.VMEM((8, 2048), BF), pltpu.SemaphoreType.DMA((CHIPS,))],
        compiler_params=LIMIT,
        name="combine",
    )(x, po, pll)


def project_kernel(a_ref, w_ref, x_ref, own_ref, other_ref):
    acc = jnp.zeros((256, 256), F32)
    top = (iota((256, 256), 0) & 7) < STEPS
    for half in range(2):
        part = jnp.zeros((256, 256), F32)
        for i in range(8):
            rows = pl.ds(half * 2048 + i * 256, 256)
            w = jnp.concatenate([w_ref[rows, :], x_ref[rows, :]], axis=1)
            part += mm(a_ref[:, pl.ds(i * 256, 256)], w)
        acc = jnp.where(top, part, acc) if half == 0 else jnp.where(top, acc, part)
    sub = iota((8, 256), 0)
    for k in range(16):
        a, b = acc[k * 16 : k * 16 + 8], acc[k * 16 + 8 : k * 16 + 16]
        a, b = a + pltpu.roll(a, STEPS, 0), b + pltpu.roll(b, STEPS, 0)
        both = jnp.where(sub < STEPS, a, b)
        own_ref[pl.ds(k * 8, 8), :] = both[:, :128]
        other_ref[pl.ds(k * 8, 8), :] = both[:, 128:]


def project(a, w, x):
    return pl.pallas_call(
        project_kernel,
        out_shape=[jax.ShapeDtypeStruct((128, 128), F32)] * 2,
        in_specs=[VM] * 3,
        out_specs=[VM] * 2,
        compiler_params=LIMIT,
        cost_estimate=pl.CostEstimate(
            flops=540_000_000, transcendentals=0, bytes_accessed=3_000_000
        ),
        name="project",
    )(a, w, x)


def order_kernel(own_ref, other_ref, out_ref):
    first = (lax.axis_index("req") & 1) == 0
    mine, theirs = own_ref[...], other_ref[...]
    even = jnp.where(first, mine, theirs)
    odd = jnp.where(first, theirs, mine)
    sub = iota((8, 128), 0)
    for k in range(16):
        a, b = even[k * 8 : k * 8 + 8], odd[k * 8 : k * 8 + 8]
        out_ref[pl.ds(k * 16, 8), :] = jnp.where(sub < STEPS, a, pltpu.roll(b, STEPS, 0))
        out_ref[pl.ds(k * 16 + 8, 8), :] = jnp.where(sub < STEPS, pltpu.roll(a, STEPS, 0), b)


def in_order(own, other):
    return pl.pallas_call(
        order_kernel,
        out_shape=jax.ShapeDtypeStruct((REQS * STEPS, 128), F32),
        in_specs=[VM] * 2,
        out_specs=VM,
        compiler_params=LIMIT,
        name="in_order",
    )(own, other)


def over_chips(x):
    return lax.all_to_all(
        x, "req", split_axis=0, concat_axis=0, axis_index_groups=SAME_CORE, tiled=True
    )


def swap_cores(x):
    return lax.ppermute(x, "req", CORE_SWAP)


def local(queries, nk, nv, pk, pv, hk, hv, kept, membership, out_weight):
    packed, own = pack(membership, queries)
    pk1, pv1, w1 = swap_cores(pk), swap_cores(pv), swap_cores(out_weight)
    q = over_chips(packed)
    po, pll = private(own, kept, hk, hv, nk, nv)
    q, po, pll = lax.optimization_barrier((q, po, pll))
    parts = over_chips(prefix(q, pk, pv, pk1, pv1))
    att = over_chips(combine(parts, po, pll))
    mine, other = project(att.reshape(256, 2048), out_weight, w1)
    part = in_order(mine, swap_cores(other))
    theirs = lax.ppermute(part, "kvh", [(0, 1), (1, 0)])
    return (part + theirs).astype(BF).reshape(REQS, STEPS, 128)


def solution(mesh):
    placed = (
        P("req", None, "kvh"),
        P("req", None, "kvh"),
        P("req", None, "kvh"),
        P(None, "req", "kvh"),
        P(None, "req", "kvh"),
        P("req", None, "kvh"),
        P("req", None, "kvh"),
        P("req", "kvh", None),
        P("req", None),
        P("kvh", "req"),
    )
    return jax.shard_map(
        local, mesh=mesh, in_specs=placed, out_specs=P(None, None, "req"), check_vma=False
    )
```

```python
import jax
import jax.numpy as jnp
from jax import lax
from jax.experimental import pallas as pl
from jax.experimental.pallas import tpu as pltpu
from jax.sharding import PartitionSpec as P

HEAD = 128
PROMPTS = 8
STEPS = 4
ROWS = 32
REQS = 64
CHIPS = 32
PORTION = 256
HISTORY = 2048
KEPT = 1024
GROUP = 4
UNROLL = 2
PAY = 136
LOG2E = 1.4426950408889634
C2 = HEAD ** -0.5 * LOG2E
NEG = -1e30
BF = jnp.bfloat16
F32 = jnp.float32

SAME_CORE = [[2 * i + c for i in range(CHIPS)] for c in range(2)]
CORE_SWAP = [(i, i ^ 1) for i in range(REQS)]

LIMIT = pltpu.CompilerParams(vmem_limit_bytes=24 << 20)

VM = pl.BlockSpec(memory_space=pltpu.VMEM)
HB = pl.BlockSpec(memory_space=pltpu.HBM)


def in_hbm(x):
    return pltpu.with_memory_space_constraint(x, pltpu.HBM)


def nt(a, b):
    return lax.dot_general(a, b, (((1,), (1,)), ((), ())), preferred_element_type=F32)


def mm(a, b):
    return lax.dot_general(a, b, (((1,), (0,)), ((), ())), preferred_element_type=F32)


def iota(shape, dim):
    return lax.broadcasted_iota(jnp.int32, shape, dim)


def spread(tile, out_ref, sem):
    copies = [pltpu.make_async_copy(tile, out_ref.at[i], sem.at[i]) for i in range(CHIPS)]
    for copy in copies:
        copy.start()
    for copy in copies:
        copy.wait()


def pack_kernel(mem_ref, q_hbm, out_ref, own_ref, q_ref, tmp, tile, sem, in_sem):
    cq = pltpu.make_async_copy(q_hbm, q_ref, in_sem)
    cq.start()
    cq.wait()
    for head in range(32):
        tmp[pl.ds(head * STEPS, STEPS), :] = q_ref[0, :, pl.ds(head * HEAD, HEAD)].astype(F32)
    data = tmp[...].astype(BF)
    own_ref[...] = data
    side = jnp.full((8, HEAD), mem_ref[0, 0], jnp.int32).astype(F32).astype(BF)
    tile[pl.ds(0, 128), :] = data
    tile[pl.ds(128, 8), :] = side
    spread(tile, out_ref, sem)


def pack(membership, queries):
    return pl.pallas_call(
        pack_kernel,
        out_shape=[
            pltpu.HBM((CHIPS, PAY, HEAD), BF),
            jax.ShapeDtypeStruct((128, HEAD), BF),
        ],
        in_specs=[pl.BlockSpec(memory_space=pltpu.SMEM), HB],
        out_specs=[HB, VM],
        scratch_shapes=[
            pltpu.VMEM((1, STEPS, 32 * HEAD), BF),
            pltpu.VMEM((128, HEAD), F32),
            pltpu.VMEM((PAY, HEAD), BF),
            pltpu.SemaphoreType.DMA((CHIPS,)),
            pltpu.SemaphoreType.DMA(()),
        ],
        compiler_params=LIMIT,
        name="pack",
    )(membership, in_hbm(queries))


def private_kernel(q_ref, kept_ref, hk_ref, hv_ref, nk_ref, nv_ref, o_ref, l_ref, knew, vnew):
    ones = jnp.ones((HISTORY, HEAD), BF)
    ones_new = jnp.ones((128, HEAD), BF)
    sub_hi = iota((16, KEPT), 0)
    sub_lo = iota((128, KEPT), 0)
    col = iota((ROWS, 128), 1)
    step_of = iota((ROWS, 128), 0) & (STEPS - 1)
    new_ok = (col < STEPS) & (col <= step_of)
    knew[...] = jnp.zeros_like(knew)
    vnew[...] = jnp.zeros_like(vnew)
    for g in range(4):
        lanes = pl.ds(g * HEAD, HEAD)
        pos = kept_ref[0, pl.ds(g, 1), :]
        hot_hi = jnp.where(sub_hi == lax.shift_right_logical(pos, 7), 1.0, 0.0).astype(BF)
        hot_lo = jnp.where(sub_lo == (pos & 127), 1.0, 0.0).astype(BF)
        count = nt(hot_hi, hot_lo)
        q = q_ref[pl.ds(g * ROWS, ROWS), :]
        s = nt(q, hk_ref[0, :, lanes])
        s = jnp.concatenate(
            [
                jnp.where(count[i : i + 1, :] > 0.5, s[:, i * 128 : (i + 1) * 128], NEG)
                for i in range(16)
            ],
            axis=1,
        )
        knew[pl.ds(0, STEPS), :] = nk_ref[0, :, lanes].astype(F32)
        vnew[pl.ds(0, STEPS), :] = nv_ref[0, :, lanes].astype(F32)
        sn = jnp.where(new_ok, nt(q, knew[...].astype(BF)), NEG)
        peak = jnp.maximum(jnp.max(s, axis=1, keepdims=True), jnp.max(sn, axis=1, keepdims=True))
        p = jnp.exp2((s - peak) * C2).astype(BF)
        pn = jnp.exp2((sn - peak) * C2).astype(BF)
        ov = mm(p, jnp.concatenate([hv_ref[0, :, lanes], ones], axis=1))
        ov += mm(pn, jnp.concatenate([vnew[...].astype(BF), ones_new], axis=1))
        total = ov[:, HEAD:]
        o_ref[g] = ov[:, :HEAD] / total
        l_ref[g] = peak * C2 + jnp.log(total) * LOG2E


def private(own, kept, hk, hv, nk, nv):
    return pl.pallas_call(
        private_kernel,
        out_shape=[jax.ShapeDtypeStruct((4, ROWS, HEAD), F32)] * 2,
        in_specs=[VM] * 6,
        out_specs=[VM] * 2,
        scratch_shapes=[pltpu.VMEM((128, HEAD), F32)] * 2,
        cost_estimate=pl.CostEstimate(
            flops=400_000_000, transcendentals=300_000, bytes_accessed=5_000_000
        ),
        compiler_params=LIMIT,
        name="private",
    )(own, kept, hk, hv, nk, nv)


def prefix_kernel(q, k0h, v0h, k1h, v1h, out_ref, k0, v0, k1, v1, lbuf, tab_v, tab_s, tsem, ksem):
    def fetch(p):
        pairs = ((k0h, k0), (v0h, v0), (k1h, k1), (v1h, v1))
        return [pltpu.make_async_copy(a.at[p], b.at[p], ksem.at[p, i]) for i, (a, b) in enumerate(pairs)]

    for p in range(PROMPTS):
        for copy in fetch(p):
            copy.start()

    sides = q[:, pl.ds(128, 8), :].astype(F32)
    member = jnp.max(sides, axis=1)
    member = jnp.concatenate([member, jnp.full((96, HEAD), 99.0, F32)], axis=0)
    across = member.T
    row, lane = iota((128, 128), 0), iota((128, 128), 1)
    before = (across < member) | ((across == member) & (lane < row))
    slot = jnp.sum(jnp.where(before, 1.0, 0.0), axis=1, keepdims=True)
    lanef = lane.astype(F32)
    here = slot == jnp.minimum(lanef, CHIPS - 1.0)

    def total(x):
        return jnp.sum(x, axis=0, keepdims=True)

    order = total(jnp.where(here, row.astype(F32), 0.0))
    counts = total(jnp.where(member == lanef, 1.0, 0.0))
    p8, l8 = iota((8, 128), 0).astype(F32), lanef[:8]
    parts = jnp.where(l8 < PROMPTS, jnp.floor((counts + (GROUP - 1.0)) * (1.0 / GROUP)), 0.0)

    def along(x):
        return jnp.sum(x, axis=1, keepdims=True)

    until = along(jnp.where(l8 <= p8, parts, 0.0))
    since = until - along(jnp.where(l8 == p8, parts, 0.0))
    starts = along(jnp.where(across[:8] < p8, 1.0, 0.0))
    groups = total(jnp.where(p8 == PROMPTS - 1.0, until, 0.0))
    at = jnp.minimum(l8, groups - 1.0)
    inside = (at >= since) & (at < until)
    prompts = total(jnp.where(inside, p8, 0.0))
    firsts = total(jnp.where(inside, starts + GROUP * (at - since), 0.0))
    table = jnp.concatenate([order, prompts, firsts, groups, jnp.zeros((4, 128), F32)], axis=0)
    tab_v[...] = table.astype(jnp.int32)
    ct = pltpu.make_async_copy(tab_v, tab_s, tsem)
    ct.start()
    ct.wait()

    ones = jnp.ones((2 * PORTION, HEAD), BF)

    def arrive(p, c):
        for copy in fetch(p):
            copy.wait()
        return c

    def several(i, seen):
        ps = [tab_s[1, i * UNROLL + u] for u in range(UNROLL)]
        lax.fori_loop(seen, ps[-1] + 1, arrive, 0)
        for u in range(UNROLL):
            p, slot0 = ps[u], tab_s[2, i * UNROLL + u]
            at = [tab_s[0, slot0 + j] for j in range(GROUP)]
            for g in range(4):
                rows, lanes = pl.ds(g * ROWS, ROWS), pl.ds(g * HEAD, HEAD)
                qs = jnp.concatenate([q[t, rows, :] for t in at], axis=0)
                s = jnp.concatenate([nt(qs, k0[p, :, lanes]), nt(qs, k1[p, :, lanes])], axis=1)
                peak = jnp.max(s, axis=1, keepdims=True)
                w = jnp.exp2((s - peak) * C2).astype(BF)
                v = jnp.concatenate([v0[p, :, lanes], v1[p, :, lanes]], axis=0)
                ov = mm(w, jnp.concatenate([v, ones], axis=1))
                l = ov[:, HEAD:]
                o = (ov[:, :HEAD] / l).astype(BF)
                lse = peak * C2 + jnp.log(l) * LOG2E
                for j in reversed(range(GROUP)):
                    out_ref[at[j], rows, :] = o[j * ROWS : (j + 1) * ROWS]
                    lbuf[at[j], rows, :] = lse[j * ROWS : (j + 1) * ROWS]
        return ps[-1] + 1

    seen = lax.fori_loop(0, (tab_s[3, 0] + UNROLL - 1) // UNROLL, several, 0)
    lax.fori_loop(seen, PROMPTS, arrive, 0)

    diag = row == lane
    sub = iota((8, 128), 0)
    for n in range(CHIPS):
        lse = total(jnp.where(diag, lbuf[n], 0.0))
        hi = lse.astype(BF).astype(F32)
        mid = (lse - hi).astype(BF).astype(F32)
        lo = lse - hi - mid
        side = jnp.where(sub == 0, hi, jnp.where(sub == 1, mid, jnp.where(sub == 2, lo, 0.0)))
        out_ref[n, pl.ds(128, 8), :] = side.astype(BF)


def prefix(q, k0, v0, k1, v1):
    return pl.pallas_call(
        prefix_kernel,
        out_shape=jax.ShapeDtypeStruct((CHIPS, PAY, HEAD), BF),
        in_specs=[VM] + [HB] * 4,
        out_specs=VM,
        scratch_shapes=[pltpu.VMEM((PROMPTS, PORTION, 512), BF)] * 4
        + [
            pltpu.VMEM((CHIPS, 128, HEAD), F32),
            pltpu.VMEM((8, 128), jnp.int32),
            pltpu.SMEM((8, 128), jnp.int32),
            pltpu.SemaphoreType.DMA(()),
            pltpu.SemaphoreType.DMA((PROMPTS, 4)),
        ],
        compiler_params=LIMIT,
        cost_estimate=pl.CostEstimate(
            flops=1_200_000_000, transcendentals=2_000_000, bytes_accessed=10_000_000
        ),
        name="prefix",
    )(q, in_hbm(k0), in_hbm(v0), k1, v1)


def combine_kernel(in_ref, po_ref, pl_ref, out_ref):
    row, lane = iota((128, 128), 0), iota((128, 128), 1)
    own = jnp.sum(jnp.where(row == lane, pl_ref[...].reshape(128, 128), 0.0), axis=0, keepdims=True)
    pieces = [in_ref[n, pl.ds(128, 8), :].astype(F32) for n in range(CHIPS)]
    lse = jnp.concatenate([x[0:1] + x[1:2] + x[2:3] for x in pieces], axis=0)
    top = jnp.maximum(jnp.max(lse, axis=0, keepdims=True), own)
    e, eo = jnp.exp2(lse - top), jnp.exp2(own - top)
    both = jnp.sum(e, axis=0, keepdims=True) + eo
    cols = jnp.concatenate([e / both, jnp.zeros((95, 128), F32), eo / both], axis=0).T
    acc = cols[:, 127:128] * po_ref[...].reshape(128, HEAD)
    for n in range(CHIPS):
        acc += cols[:, n : n + 1] * in_ref[n, pl.ds(0, 128), :].astype(F32)
    sub = iota((8, 128), 0)
    tiles = []
    for j in range(16):
        g, h = j // 8, j % 8
        a = acc[g * ROWS + h // 2 * 8 : g * ROWS + h // 2 * 8 + 8]
        b = acc[(g + 2) * ROWS + h // 2 * 8 : (g + 2) * ROWS + h // 2 * 8 + 8]
        if h % 2 == 0:
            tiles.append(jnp.where(sub < STEPS, a, pltpu.roll(b, STEPS, 0)))
        else:
            tiles.append(jnp.where(sub < STEPS, pltpu.roll(a, STEPS, 0), b))
    att = jnp.concatenate(tiles, axis=1).astype(BF)
    for n in range(CHIPS):
        out_ref[n] = att


def combine(x, po, pll):
    return pl.pallas_call(
        combine_kernel,
        out_shape=jax.ShapeDtypeStruct((CHIPS, 8, 2048), BF),
        in_specs=[VM] * 3,
        out_specs=VM,
        compiler_params=LIMIT,
        name="combine",
    )(x, po, pll)


def project_kernel(a_ref, w_ref, x_ref, own_ref, other_ref):
    acc = jnp.zeros((256, 256), F32)
    top = (iota((256, 256), 0) & 7) < STEPS
    for half in range(2):
        part = jnp.zeros((256, 256), F32)
        for i in range(8):
            rows = pl.ds(half * 2048 + i * 256, 256)
            w = jnp.concatenate([w_ref[rows, :], x_ref[rows, :]], axis=1)
            part += mm(a_ref[:, pl.ds(i * 256, 256)], w)
        acc = jnp.where(top, part, acc) if half == 0 else jnp.where(top, acc, part)
    sub = iota((8, 256), 0)
    for k in range(16):
        a, b = acc[k * 16 : k * 16 + 8], acc[k * 16 + 8 : k * 16 + 16]
        a, b = a + pltpu.roll(a, STEPS, 0), b + pltpu.roll(b, STEPS, 0)
        both = jnp.where(sub < STEPS, a, b)
        own_ref[pl.ds(k * 8, 8), :] = both[:, :128]
        other_ref[pl.ds(k * 8, 8), :] = both[:, 128:]


def project(a, w, x):
    return pl.pallas_call(
        project_kernel,
        out_shape=[jax.ShapeDtypeStruct((128, 128), F32)] * 2,
        in_specs=[VM] * 3,
        out_specs=[VM] * 2,
        compiler_params=LIMIT,
        cost_estimate=pl.CostEstimate(
            flops=540_000_000, transcendentals=0, bytes_accessed=3_000_000
        ),
        name="project",
    )(a, w, x)


def order_kernel(own_ref, other_ref, out_ref):
    first = (lax.axis_index("req") & 1) == 0
    mine, theirs = own_ref[...], other_ref[...]
    even = jnp.where(first, mine, theirs)
    odd = jnp.where(first, theirs, mine)
    sub = iota((8, 128), 0)
    for k in range(16):
        a, b = even[k * 8 : k * 8 + 8], odd[k * 8 : k * 8 + 8]
        out_ref[pl.ds(k * 16, 8), :] = jnp.where(sub < STEPS, a, pltpu.roll(b, STEPS, 0))
        out_ref[pl.ds(k * 16 + 8, 8), :] = jnp.where(sub < STEPS, pltpu.roll(a, STEPS, 0), b)


def in_order(own, other):
    return pl.pallas_call(
        order_kernel,
        out_shape=jax.ShapeDtypeStruct((REQS * STEPS, 128), F32),
        in_specs=[VM] * 2,
        out_specs=VM,
        compiler_params=LIMIT,
        name="in_order",
    )(own, other)


def over_chips(x):
    return lax.all_to_all(
        x, "req", split_axis=0, concat_axis=0, axis_index_groups=SAME_CORE, tiled=True
    )


def swap_cores(x):
    return lax.ppermute(x, "req", CORE_SWAP)


def local(queries, nk, nv, pk, pv, hk, hv, kept, membership, out_weight):
    packed, own = pack(membership, queries)
    pk1, pv1, w1 = swap_cores(pk), swap_cores(pv), swap_cores(out_weight)
    q = over_chips(packed)
    po, pll = private(own, kept, hk, hv, nk, nv)
    q, po, pll, w1 = lax.optimization_barrier((q, po, pll, w1))
    parts = over_chips(prefix(q, pk, pv, pk1, pv1))
    att = over_chips(combine(parts, po, pll))
    mine, other = project(att.reshape(256, 2048), out_weight, w1)
    part = in_order(mine, swap_cores(other))
    theirs = lax.ppermute(part, "kvh", [(0, 1), (1, 0)])
    return (part + theirs).astype(BF).reshape(REQS, STEPS, 128)


def solution(mesh):
    placed = (
        P("req", None, "kvh"),
        P("req", None, "kvh"),
        P("req", None, "kvh"),
        P(None, "req", "kvh"),
        P(None, "req", "kvh"),
        P("req", None, "kvh"),
        P("req", None, "kvh"),
        P("req", "kvh", None),
        P("req", None),
        P("kvh", "req"),
    )
    return jax.shard_map(
        local, mesh=mesh, in_specs=placed, out_specs=P(None, None, "req"), check_vma=False
    )
```

```python
import jax
import jax.numpy as jnp
from jax import lax
from jax.experimental import pallas as pl
from jax.experimental.pallas import tpu as pltpu
from jax.sharding import PartitionSpec as P


HEAD = 128
PROMPTS = 8
STEPS = 4
ROWS = 32
REQS = 64
CHIPS = 32
PORTION = 256
HISTORY = 2048
KEPT = 1024
GROUP = 4
UNROLL = 4
PAY = 136
LOG2E = 1.4426950408889634
C2 = HEAD ** -0.5 * LOG2E
NEG = -1e30
BF = jnp.bfloat16
F32 = jnp.float32

SAME_CORE = [[2 * i + c for i in range(CHIPS)] for c in range(2)]
CORE_SWAP = [(i, i ^ 1) for i in range(REQS)]

LIMIT = pltpu.CompilerParams(vmem_limit_bytes=24 << 20)

VM = pl.BlockSpec(memory_space=pltpu.VMEM)
HB = pl.BlockSpec(memory_space=pltpu.HBM)


def in_hbm(x):
    return pltpu.with_memory_space_constraint(x, pltpu.HBM)


def nt(a, b):
    return lax.dot_general(a, b, (((1,), (1,)), ((), ())), preferred_element_type=F32)


def mm(a, b):
    return lax.dot_general(a, b, (((1,), (0,)), ((), ())), preferred_element_type=F32)


def iota(shape, dim):
    return lax.broadcasted_iota(jnp.int32, shape, dim)


def pack_kernel(mem_ref, q_hbm, out_ref, own_ref, q_ref, tmp, tile, sem, in_sem):
    cq = pltpu.make_async_copy(q_hbm, q_ref, in_sem)
    cq.start()
    cq.wait()
    for head in range(32):
        tmp[pl.ds(head * STEPS, STEPS), :] = q_ref[0, :, pl.ds(head * HEAD, HEAD)].astype(F32)
    data = tmp[...].astype(BF)
    own_ref[...] = data
    side = jnp.full((8, HEAD), mem_ref[0, 0], jnp.int32).astype(F32).astype(BF)
    for i in range(CHIPS):
        tile[i, pl.ds(0, 128), :] = data
        tile[i, pl.ds(128, 8), :] = side
    copy = pltpu.make_async_copy(tile, out_ref, sem)
    copy.start()
    copy.wait()


def pack(membership, queries):
    return pl.pallas_call(
        pack_kernel,
        out_shape=[
            pltpu.HBM((CHIPS, PAY, HEAD), BF),
            jax.ShapeDtypeStruct((128, HEAD), BF),
        ],
        in_specs=[pl.BlockSpec(memory_space=pltpu.SMEM), HB],
        out_specs=[HB, VM],
        scratch_shapes=[
            pltpu.VMEM((1, STEPS, 32 * HEAD), BF),
            pltpu.VMEM((128, HEAD), F32),
            pltpu.VMEM((CHIPS, PAY, HEAD), BF),
            pltpu.SemaphoreType.DMA(()),
            pltpu.SemaphoreType.DMA(()),
        ],
        compiler_params=LIMIT,
        name="pack",
    )(membership, in_hbm(queries))


def private_kernel(q_ref, kept_ref, hk_ref, hv_ref, nk_ref, nv_ref, o_ref, l_ref, knew, vnew):
    ones = jnp.ones((HISTORY, HEAD), BF)
    ones_new = jnp.ones((128, HEAD), BF)
    sub_hi = iota((16, KEPT), 0)
    sub_lo = iota((128, KEPT), 0)
    col = iota((ROWS, 128), 1)
    step_of = iota((ROWS, 128), 0) & (STEPS - 1)
    new_ok = (col < STEPS) & (col <= step_of)
    knew[...] = jnp.zeros_like(knew)
    vnew[...] = jnp.zeros_like(vnew)
    for g in range(4):
        lanes = pl.ds(g * HEAD, HEAD)
        pos = kept_ref[0, pl.ds(g, 1), :]
        hot_hi = jnp.where(sub_hi == lax.shift_right_logical(pos, 7), 1.0, 0.0).astype(BF)
        hot_lo = jnp.where(sub_lo == (pos & 127), 1.0, 0.0).astype(BF)
        count = nt(hot_hi, hot_lo)
        q = q_ref[pl.ds(g * ROWS, ROWS), :]
        s = nt(q, hk_ref[0, :, lanes])
        s = jnp.concatenate(
            [
                jnp.where(count[i : i + 1, :] > 0.5, s[:, i * 128 : (i + 1) * 128], NEG)
                for i in range(16)
            ],
            axis=1,
        )
        knew[pl.ds(0, STEPS), :] = nk_ref[0, :, lanes].astype(F32)
        vnew[pl.ds(0, STEPS), :] = nv_ref[0, :, lanes].astype(F32)
        sn = jnp.where(new_ok, nt(q, knew[...].astype(BF)), NEG)
        peak = jnp.maximum(jnp.max(s, axis=1, keepdims=True), jnp.max(sn, axis=1, keepdims=True))
        p = jnp.exp2((s - peak) * C2).astype(BF)
        pn = jnp.exp2((sn - peak) * C2).astype(BF)
        ov = mm(p, jnp.concatenate([hv_ref[0, :, lanes], ones], axis=1))
        ov += mm(pn, jnp.concatenate([vnew[...].astype(BF), ones_new], axis=1))
        total = ov[:, HEAD:]
        o_ref[g] = ov[:, :HEAD] / total
        l_ref[g] = peak * C2 + jnp.log(total) * LOG2E


def private(own, kept, hk, hv, nk, nv):
    return pl.pallas_call(
        private_kernel,
        out_shape=[jax.ShapeDtypeStruct((4, ROWS, HEAD), F32)] * 2,
        in_specs=[VM] * 6,
        out_specs=[VM] * 2,
        scratch_shapes=[pltpu.VMEM((128, HEAD), F32)] * 2,
        cost_estimate=pl.CostEstimate(
            flops=400_000_000, transcendentals=300_000, bytes_accessed=5_000_000
        ),
        compiler_params=LIMIT,
        name="private",
    )(own, kept, hk, hv, nk, nv)


def prefix_kernel(q, k0h, v0h, k1h, v1h, out_ref, k0, v0, k1, v1, lbuf, tab_v, tab_s, tsem, ksem):
    def fetch(p):
        pairs = ((k0h, k0), (v0h, v0), (k1h, k1), (v1h, v1))
        return [pltpu.make_async_copy(a.at[p], b.at[p], ksem.at[p, i]) for i, (a, b) in enumerate(pairs)]

    for p in range(PROMPTS):
        for copy in fetch(p):
            copy.start()

    sides = q[:, pl.ds(128, 8), :].astype(F32)
    member = jnp.max(sides, axis=1)
    member = jnp.concatenate([member, jnp.full((96, HEAD), 99.0, F32)], axis=0)
    across = member.T
    row, lane = iota((128, 128), 0), iota((128, 128), 1)
    before = (across < member) | ((across == member) & (lane < row))
    slot = jnp.sum(jnp.where(before, 1.0, 0.0), axis=1, keepdims=True)
    lanef = lane.astype(F32)
    here = slot == jnp.minimum(lanef, CHIPS - 1.0)

    def total(x):
        return jnp.sum(x, axis=0, keepdims=True)

    order = total(jnp.where(here, row.astype(F32), 0.0))
    counts = total(jnp.where(member == lanef, 1.0, 0.0))
    p8, l8 = iota((8, 128), 0).astype(F32), lanef[:8]
    parts = jnp.where(l8 < PROMPTS, jnp.floor((counts + (GROUP - 1.0)) * (1.0 / GROUP)), 0.0)

    def along(x):
        return jnp.sum(x, axis=1, keepdims=True)

    until = along(jnp.where(l8 <= p8, parts, 0.0))
    since = until - along(jnp.where(l8 == p8, parts, 0.0))
    starts = along(jnp.where(across[:8] < p8, 1.0, 0.0))
    groups = total(jnp.where(p8 == PROMPTS - 1.0, until, 0.0))
    at = jnp.minimum(l8, groups - 1.0)
    inside = (at >= since) & (at < until)
    prompts = total(jnp.where(inside, p8, 0.0))
    firsts = total(jnp.where(inside, starts + GROUP * (at - since), 0.0))
    table = jnp.concatenate([order, prompts, firsts, groups, jnp.zeros((4, 128), F32)], axis=0)
    tab_v[...] = table.astype(jnp.int32)
    ct = pltpu.make_async_copy(tab_v, tab_s, tsem)
    ct.start()
    ct.wait()

    ones = jnp.ones((2 * PORTION, HEAD), BF)

    def arrive(p, c):
        for copy in fetch(p):
            copy.wait()
        return c

    def several(i, seen):
        ps = [tab_s[1, i * UNROLL + u] for u in range(UNROLL)]
        lax.fori_loop(seen, ps[-1] + 1, arrive, 0)
        for u in range(UNROLL):
            p, slot0 = ps[u], tab_s[2, i * UNROLL + u]
            at = [tab_s[0, slot0 + j] for j in range(GROUP)]
            for g in range(4):
                rows, lanes = pl.ds(g * ROWS, ROWS), pl.ds(g * HEAD, HEAD)
                qs = jnp.concatenate([q[t, rows, :] for t in at], axis=0)
                s = jnp.concatenate([nt(qs, k0[p, :, lanes]), nt(qs, k1[p, :, lanes])], axis=1)
                peak = jnp.max(s, axis=1, keepdims=True)
                w = jnp.exp2((s - peak) * C2).astype(BF)
                v = jnp.concatenate([v0[p, :, lanes], v1[p, :, lanes]], axis=0)
                ov = mm(w, jnp.concatenate([v, ones], axis=1))
                l = ov[:, HEAD:]
                o = (ov[:, :HEAD] / l).astype(BF)
                lse = peak * C2 + jnp.log(l) * LOG2E
                for j in reversed(range(GROUP)):
                    out_ref[at[j], rows, :] = o[j * ROWS : (j + 1) * ROWS]
                    lbuf[at[j], rows, :] = lse[j * ROWS : (j + 1) * ROWS]
        return ps[-1] + 1

    seen = lax.fori_loop(0, (tab_s[3, 0] + UNROLL - 1) // UNROLL, several, 0)
    lax.fori_loop(seen, PROMPTS, arrive, 0)

    diag = row == lane
    sub = iota((8, 128), 0)
    for n in range(CHIPS):
        lse = total(jnp.where(diag, lbuf[n], 0.0))
        hi = lse.astype(BF).astype(F32)
        mid = (lse - hi).astype(BF).astype(F32)
        lo = lse - hi - mid
        side = jnp.where(sub == 0, hi, jnp.where(sub == 1, mid, jnp.where(sub == 2, lo, 0.0)))
        out_ref[n, pl.ds(128, 8), :] = side.astype(BF)


def prefix(q, k0, v0, k1, v1):
    return pl.pallas_call(
        prefix_kernel,
        out_shape=jax.ShapeDtypeStruct((CHIPS, PAY, HEAD), BF),
        in_specs=[VM] + [HB] * 4,
        out_specs=VM,
        scratch_shapes=[pltpu.VMEM((PROMPTS, PORTION, 512), BF)] * 4
        + [
            pltpu.VMEM((CHIPS, 128, HEAD), F32),
            pltpu.VMEM((8, 128), jnp.int32),
            pltpu.SMEM((8, 128), jnp.int32),
            pltpu.SemaphoreType.DMA(()),
            pltpu.SemaphoreType.DMA((PROMPTS, 4)),
        ],
        compiler_params=LIMIT,
        cost_estimate=pl.CostEstimate(
            flops=1_200_000_000, transcendentals=2_000_000, bytes_accessed=10_000_000
        ),
        name="prefix",
    )(q, in_hbm(k0), in_hbm(v0), k1, v1)


def combine_kernel(in_ref, po_ref, pl_ref, out_ref):
    row, lane = iota((128, 128), 0), iota((128, 128), 1)
    own = jnp.sum(jnp.where(row == lane, pl_ref[...].reshape(128, 128), 0.0), axis=0, keepdims=True)
    pieces = [in_ref[n, pl.ds(128, 8), :].astype(F32) for n in range(CHIPS)]
    lse = jnp.concatenate([x[0:1] + x[1:2] + x[2:3] for x in pieces], axis=0)
    top = jnp.maximum(jnp.max(lse, axis=0, keepdims=True), own)
    e, eo = jnp.exp2(lse - top), jnp.exp2(own - top)
    both = jnp.sum(e, axis=0, keepdims=True) + eo
    cols = jnp.concatenate([e / both, jnp.zeros((95, 128), F32), eo / both], axis=0).T
    acc = cols[:, 127:128] * po_ref[...].reshape(128, HEAD)
    for n in range(CHIPS):
        acc += cols[:, n : n + 1] * in_ref[n, pl.ds(0, 128), :].astype(F32)
    sub = iota((8, 128), 0)
    tiles = []
    for j in range(16):
        g, h = j // 8, j % 8
        a = acc[g * ROWS + h // 2 * 8 : g * ROWS + h // 2 * 8 + 8]
        b = acc[(g + 2) * ROWS + h // 2 * 8 : (g + 2) * ROWS + h // 2 * 8 + 8]
        if h % 2 == 0:
            tiles.append(jnp.where(sub < STEPS, a, pltpu.roll(b, STEPS, 0)))
        else:
            tiles.append(jnp.where(sub < STEPS, pltpu.roll(a, STEPS, 0), b))
    att = jnp.concatenate(tiles, axis=1).astype(BF)
    for n in range(CHIPS):
        out_ref[n] = att


def combine(x, po, pll):
    return pl.pallas_call(
        combine_kernel,
        out_shape=jax.ShapeDtypeStruct((CHIPS, 8, 2048), BF),
        in_specs=[VM] * 3,
        out_specs=VM,
        compiler_params=LIMIT,
        name="combine",
    )(x, po, pll)


def project_kernel(a_ref, w_ref, x_ref, own_ref, other_ref):
    acc = jnp.zeros((256, 256), F32)
    top = (iota((256, 256), 0) & 7) < STEPS
    for half in range(2):
        part = jnp.zeros((256, 256), F32)
        for i in range(8):
            rows = pl.ds(half * 2048 + i * 256, 256)
            w = jnp.concatenate([w_ref[rows, :], x_ref[rows, :]], axis=1)
            part += mm(a_ref[:, pl.ds(i * 256, 256)], w)
        acc = jnp.where(top, part, acc) if half == 0 else jnp.where(top, acc, part)
    sub = iota((8, 256), 0)
    for k in range(16):
        a, b = acc[k * 16 : k * 16 + 8], acc[k * 16 + 8 : k * 16 + 16]
        a, b = a + pltpu.roll(a, STEPS, 0), b + pltpu.roll(b, STEPS, 0)
        both = jnp.where(sub < STEPS, a, b)
        own_ref[pl.ds(k * 8, 8), :] = both[:, :128]
        other_ref[pl.ds(k * 8, 8), :] = both[:, 128:]


def project(a, w, x):
    return pl.pallas_call(
        project_kernel,
        out_shape=[jax.ShapeDtypeStruct((128, 128), F32)] * 2,
        in_specs=[VM] * 3,
        out_specs=[VM] * 2,
        compiler_params=LIMIT,
        cost_estimate=pl.CostEstimate(
            flops=540_000_000, transcendentals=0, bytes_accessed=3_000_000
        ),
        name="project",
    )(a, w, x)


def order_kernel(own_ref, other_ref, out_ref):
    first = (lax.axis_index("req") & 1) == 0
    mine, theirs = own_ref[...], other_ref[...]
    even = jnp.where(first, mine, theirs)
    odd = jnp.where(first, theirs, mine)
    sub = iota((8, 128), 0)
    for k in range(16):
        a, b = even[k * 8 : k * 8 + 8], odd[k * 8 : k * 8 + 8]
        out_ref[pl.ds(k * 16, 8), :] = jnp.where(sub < STEPS, a, pltpu.roll(b, STEPS, 0))
        out_ref[pl.ds(k * 16 + 8, 8), :] = jnp.where(sub < STEPS, pltpu.roll(a, STEPS, 0), b)


def in_order(own, other):
    return pl.pallas_call(
        order_kernel,
        out_shape=jax.ShapeDtypeStruct((REQS * STEPS, 128), F32),
        in_specs=[VM] * 2,
        out_specs=VM,
        compiler_params=LIMIT,
        name="in_order",
    )(own, other)


def over_chips(x):
    return lax.all_to_all(
        x, "req", split_axis=0, concat_axis=0, axis_index_groups=SAME_CORE, tiled=True
    )


def swap_cores(x):
    return lax.ppermute(x, "req", CORE_SWAP)


def local(queries, nk, nv, pk, pv, hk, hv, kept, membership, out_weight):
    packed, own = pack(membership, queries)
    pk1, pv1, w1 = swap_cores(pk), swap_cores(pv), swap_cores(out_weight)
    q = over_chips(packed)
    po, pll = private(own, kept, hk, hv, nk, nv)
    q, po, pll, w1 = lax.optimization_barrier((q, po, pll, w1))
    parts = over_chips(prefix(q, pk, pv, pk1, pv1))
    att = over_chips(combine(parts, po, pll))
    mine, other = project(att.reshape(256, 2048), out_weight, w1)
    part = in_order(mine, swap_cores(other))
    theirs = lax.ppermute(part, "kvh", [(0, 1), (1, 0)])
    return (part + theirs).astype(BF).reshape(REQS, STEPS, 128)


def solution(mesh):
    placed = (
        P("req", None, "kvh"),
        P("req", None, "kvh"),
        P("req", None, "kvh"),
        P(None, "req", "kvh"),
        P(None, "req", "kvh"),
        P("req", None, "kvh"),
        P("req", None, "kvh"),
        P("req", "kvh", None),
        P("req", None),
        P("kvh", "req"),
    )
    return jax.shard_map(
        local, mesh=mesh, in_specs=placed, out_specs=P(None, None, "req"), check_vma=False
    )
```

```python
import jax
import jax.numpy as jnp
from jax import lax
from jax.experimental import pallas as pl
from jax.experimental.pallas import tpu as pltpu
from jax.sharding import PartitionSpec as P


HEAD = 128
PROMPTS = 8
STEPS = 4
ROWS = 32
REQS = 64
CHIPS = 32
PORTION = 256
HISTORY = 2048
KEPT = 1024
GROUP = 4
UNROLL = 4
PAY = 136
LOG2E = 1.4426950408889634
C2 = HEAD ** -0.5 * LOG2E
NEG = -1e30
BF = jnp.bfloat16
F32 = jnp.float32

SAME_CORE = [[2 * i + c for i in range(CHIPS)] for c in range(2)]
CORE_SWAP = [(i, i ^ 1) for i in range(REQS)]

LIMIT = pltpu.CompilerParams(vmem_limit_bytes=24 << 20)

VM = pl.BlockSpec(memory_space=pltpu.VMEM)
HB = pl.BlockSpec(memory_space=pltpu.HBM)


def in_hbm(x):
    return pltpu.with_memory_space_constraint(x, pltpu.HBM)


def nt(a, b):
    return lax.dot_general(a, b, (((1,), (1,)), ((), ())), preferred_element_type=F32)


def mm(a, b):
    return lax.dot_general(a, b, (((1,), (0,)), ((), ())), preferred_element_type=F32)


def iota(shape, dim):
    return lax.broadcasted_iota(jnp.int32, shape, dim)


def pack_kernel(mem_ref, q_hbm, out_ref, own_ref, q_ref, tmp, tile, sem, in_sem):
    cq = pltpu.make_async_copy(q_hbm, q_ref, in_sem)
    cq.start()
    cq.wait()
    for head in range(32):
        tmp[pl.ds(head * STEPS, STEPS), :] = q_ref[0, :, pl.ds(head * HEAD, HEAD)].astype(F32)
    data = tmp[...].astype(BF)
    own_ref[...] = data
    side = jnp.full((8, HEAD), mem_ref[0, 0], jnp.int32).astype(F32).astype(BF)
    for i in range(CHIPS):
        tile[i, pl.ds(0, 128), :] = data
        tile[i, pl.ds(128, 8), :] = side
    copy = pltpu.make_async_copy(tile, out_ref, sem)
    copy.start()
    copy.wait()


def pack(membership, queries):
    return pl.pallas_call(
        pack_kernel,
        out_shape=[
            pltpu.HBM((CHIPS, PAY, HEAD), BF),
            jax.ShapeDtypeStruct((128, HEAD), BF),
        ],
        in_specs=[pl.BlockSpec(memory_space=pltpu.SMEM), HB],
        out_specs=[HB, VM],
        scratch_shapes=[
            pltpu.VMEM((1, STEPS, 32 * HEAD), BF),
            pltpu.VMEM((128, HEAD), F32),
            pltpu.VMEM((CHIPS, PAY, HEAD), BF),
            pltpu.SemaphoreType.DMA(()),
            pltpu.SemaphoreType.DMA(()),
        ],
        compiler_params=LIMIT,
        name="pack",
    )(membership, in_hbm(queries))


def private_kernel(q_ref, kept_ref, hk_ref, hv_ref, nk_ref, nv_ref, o_ref, l_ref, knew, vnew):
    ones = jnp.ones((HISTORY, HEAD), BF)
    ones_new = jnp.ones((128, HEAD), BF)
    sub_hi = iota((16, KEPT), 0)
    sub_lo = iota((128, KEPT), 0)
    col = iota((ROWS, 128), 1)
    step_of = iota((ROWS, 128), 0) & (STEPS - 1)
    new_ok = (col < STEPS) & (col <= step_of)
    knew[...] = jnp.zeros_like(knew)
    vnew[...] = jnp.zeros_like(vnew)
    for g in range(4):
        lanes = pl.ds(g * HEAD, HEAD)
        pos = kept_ref[0, pl.ds(g, 1), :]
        hot_hi = jnp.where(sub_hi == lax.shift_right_logical(pos, 7), 1.0, 0.0).astype(BF)
        hot_lo = jnp.where(sub_lo == (pos & 127), 1.0, 0.0).astype(BF)
        count = nt(hot_hi, hot_lo)
        q = q_ref[pl.ds(g * ROWS, ROWS), :]
        s = nt(q, hk_ref[0, :, lanes])
        s = jnp.concatenate(
            [
                jnp.where(count[i : i + 1, :] > 0.5, s[:, i * 128 : (i + 1) * 128], NEG)
                for i in range(16)
            ],
            axis=1,
        )
        knew[pl.ds(0, STEPS), :] = nk_ref[0, :, lanes].astype(F32)
        vnew[pl.ds(0, STEPS), :] = nv_ref[0, :, lanes].astype(F32)
        sn = jnp.where(new_ok, nt(q, knew[...].astype(BF)), NEG)
        peak = jnp.maximum(jnp.max(s, axis=1, keepdims=True), jnp.max(sn, axis=1, keepdims=True))
        p = jnp.exp2((s - peak) * C2).astype(BF)
        pn = jnp.exp2((sn - peak) * C2).astype(BF)
        ov = mm(p, jnp.concatenate([hv_ref[0, :, lanes], ones], axis=1))
        ov += mm(pn, jnp.concatenate([vnew[...].astype(BF), ones_new], axis=1))
        total = ov[:, HEAD:]
        o_ref[g] = ov[:, :HEAD] / total
        l_ref[g] = peak * C2 + jnp.log(total) * LOG2E


def private(own, kept, hk, hv, nk, nv):
    return pl.pallas_call(
        private_kernel,
        out_shape=[jax.ShapeDtypeStruct((4, ROWS, HEAD), F32)] * 2,
        in_specs=[VM] * 6,
        out_specs=[VM] * 2,
        scratch_shapes=[pltpu.VMEM((128, HEAD), F32)] * 2,
        cost_estimate=pl.CostEstimate(
            flops=400_000_000, transcendentals=300_000, bytes_accessed=5_000_000
        ),
        compiler_params=LIMIT,
        name="private",
    )(own, kept, hk, hv, nk, nv)


def prefix_kernel(q, k0h, v0h, k1h, v1h, out_ref, k0, v0, k1, v1, lbuf, tab_v, tab_s, tsem, ksem):
    def fetch(p):
        pairs = ((k0h, k0), (v0h, v0), (k1h, k1), (v1h, v1))
        return [pltpu.make_async_copy(a.at[p], b.at[p], ksem.at[p, i]) for i, (a, b) in enumerate(pairs)]

    for p in range(PROMPTS):
        for copy in fetch(p):
            copy.start()

    sides = q[:, pl.ds(128, 8), :].astype(F32)
    member = jnp.max(sides, axis=1)
    member = jnp.concatenate([member, jnp.full((96, HEAD), 99.0, F32)], axis=0)
    across = member.T
    row, lane = iota((128, 128), 0), iota((128, 128), 1)
    before = (across < member) | ((across == member) & (lane < row))
    slot = jnp.sum(jnp.where(before, 1.0, 0.0), axis=1, keepdims=True)
    lanef = lane.astype(F32)
    here = slot == jnp.minimum(lanef, CHIPS - 1.0)

    def total(x):
        return jnp.sum(x, axis=0, keepdims=True)

    order = total(jnp.where(here, row.astype(F32), 0.0))
    counts = total(jnp.where(member == lanef, 1.0, 0.0))
    p8, l8 = iota((8, 128), 0).astype(F32), lanef[:8]
    parts = jnp.where(l8 < PROMPTS, jnp.floor((counts + (GROUP - 1.0)) * (1.0 / GROUP)), 0.0)

    def along(x):
        return jnp.sum(x, axis=1, keepdims=True)

    until = along(jnp.where(l8 <= p8, parts, 0.0))
    since = until - along(jnp.where(l8 == p8, parts, 0.0))
    starts = along(jnp.where(across[:8] < p8, 1.0, 0.0))
    groups = total(jnp.where(p8 == PROMPTS - 1.0, until, 0.0))
    at = jnp.minimum(l8, groups - 1.0)
    inside = (at >= since) & (at < until)
    prompts = total(jnp.where(inside, p8, 0.0))
    firsts = total(jnp.where(inside, starts + GROUP * (at - since), 0.0))
    table = jnp.concatenate([order, prompts, firsts, groups, jnp.zeros((4, 128), F32)], axis=0)
    tab_v[...] = table.astype(jnp.int32)
    ct = pltpu.make_async_copy(tab_v, tab_s, tsem)
    ct.start()
    ct.wait()

    ones = jnp.ones((2 * PORTION, HEAD), BF)

    def arrive(p, c):
        for copy in fetch(p):
            copy.wait()
        return c

    def several(i, seen):
        ps = [tab_s[1, i * UNROLL + u] for u in range(UNROLL)]
        lax.fori_loop(seen, ps[-1] + 1, arrive, 0)
        for u in range(UNROLL):
            p, slot0 = ps[u], tab_s[2, i * UNROLL + u]
            at = [tab_s[0, slot0 + j] for j in range(GROUP)]
            for g in range(4):
                rows, lanes = pl.ds(g * ROWS, ROWS), pl.ds(g * HEAD, HEAD)
                qs = jnp.concatenate([q[t, rows, :] for t in at], axis=0)
                s = jnp.concatenate([nt(qs, k0[p, :, lanes]), nt(qs, k1[p, :, lanes])], axis=1)
                peak = jnp.max(s, axis=1, keepdims=True)
                w = jnp.exp2((s - peak) * C2).astype(BF)
                v = jnp.concatenate([v0[p, :, lanes], v1[p, :, lanes]], axis=0)
                ov = mm(w, jnp.concatenate([v, ones], axis=1))
                l = ov[:, HEAD:]
                o = (ov[:, :HEAD] / l).astype(BF)
                lse = peak * C2 + jnp.log(l) * LOG2E
                for j in reversed(range(GROUP)):
                    out_ref[at[j], rows, :] = o[j * ROWS : (j + 1) * ROWS]
                    lbuf[at[j], rows, :] = lse[j * ROWS : (j + 1) * ROWS]
        return ps[-1] + 1

    seen = lax.fori_loop(0, (tab_s[3, 0] + UNROLL - 1) // UNROLL, several, 0)
    lax.fori_loop(seen, PROMPTS, arrive, 0)

    diag = row == lane
    sub = iota((8, 128), 0)
    for n in range(CHIPS):
        lse = total(jnp.where(diag, lbuf[n], 0.0))
        hi = lse.astype(BF).astype(F32)
        mid = (lse - hi).astype(BF).astype(F32)
        lo = lse - hi - mid
        side = jnp.where(sub == 0, hi, jnp.where(sub == 1, mid, jnp.where(sub == 2, lo, 0.0)))
        out_ref[n, pl.ds(128, 8), :] = side.astype(BF)


def prefix(q, k0, v0, k1, v1):
    return pl.pallas_call(
        prefix_kernel,
        out_shape=jax.ShapeDtypeStruct((CHIPS, PAY, HEAD), BF),
        in_specs=[VM] + [HB] * 4,
        out_specs=VM,
        scratch_shapes=[pltpu.VMEM((PROMPTS, PORTION, 512), BF)] * 4
        + [
            pltpu.VMEM((CHIPS, 128, HEAD), F32),
            pltpu.VMEM((8, 128), jnp.int32),
            pltpu.SMEM((8, 128), jnp.int32),
            pltpu.SemaphoreType.DMA(()),
            pltpu.SemaphoreType.DMA((PROMPTS, 4)),
        ],
        compiler_params=LIMIT,
        cost_estimate=pl.CostEstimate(
            flops=1_200_000_000, transcendentals=2_000_000, bytes_accessed=10_000_000
        ),
        name="prefix",
    )(q, in_hbm(k0), in_hbm(v0), k1, v1)


def combine_kernel(in_ref, po_ref, pl_ref, out_ref):
    row, lane = iota((128, 128), 0), iota((128, 128), 1)
    own = jnp.sum(jnp.where(row == lane, pl_ref[...].reshape(128, 128), 0.0), axis=0, keepdims=True)
    pieces = [in_ref[n, pl.ds(128, 8), :].astype(F32) for n in range(CHIPS)]
    lse = jnp.concatenate([x[0:1] + x[1:2] + x[2:3] for x in pieces], axis=0)
    top = jnp.maximum(jnp.max(lse, axis=0, keepdims=True), own)
    e, eo = jnp.exp2(lse - top), jnp.exp2(own - top)
    both = jnp.sum(e, axis=0, keepdims=True) + eo
    cols = jnp.concatenate([e / both, jnp.zeros((95, 128), F32), eo / both], axis=0).T
    acc = cols[:, 127:128] * po_ref[...].reshape(128, HEAD)
    for n in range(CHIPS):
        acc += cols[:, n : n + 1] * in_ref[n, pl.ds(0, 128), :].astype(F32)
    sub = iota((8, 128), 0)
    tiles = []
    for j in range(16):
        g, h = j // 8, j % 8
        a = acc[g * ROWS + h // 2 * 8 : g * ROWS + h // 2 * 8 + 8]
        b = acc[(g + 2) * ROWS + h // 2 * 8 : (g + 2) * ROWS + h // 2 * 8 + 8]
        if h % 2 == 0:
            tiles.append(jnp.where(sub < STEPS, a, pltpu.roll(b, STEPS, 0)))
        else:
            tiles.append(jnp.where(sub < STEPS, pltpu.roll(a, STEPS, 0), b))
    att = jnp.concatenate(tiles, axis=1).astype(BF)
    for n in range(CHIPS):
        out_ref[n] = att


def combine(x, po, pll):
    return pl.pallas_call(
        combine_kernel,
        out_shape=jax.ShapeDtypeStruct((CHIPS, 8, 2048), BF),
        in_specs=[VM] * 3,
        out_specs=VM,
        compiler_params=LIMIT,
        name="combine",
    )(x, po, pll)


def project_kernel(a_ref, w_ref, out_ref):
    parts = []
    for half in range(2):
        part = jnp.zeros((256, 128), F32)
        for i in range(8):
            w = w_ref[pl.ds(half * 2048 + i * 256, 256), :]
            part += mm(a_ref[:, pl.ds(i * 256, 256)], w)
        parts.append(part)
    acc = jnp.where((iota((256, 128), 0) & 7) < STEPS, parts[0], parts[1])
    sub = iota((8, 128), 0)
    for k in range(16):
        a, b = acc[k * 16 : k * 16 + 8], acc[k * 16 + 8 : k * 16 + 16]
        a, b = a + pltpu.roll(a, STEPS, 0), b + pltpu.roll(b, STEPS, 0)
        out_ref[pl.ds(k * 8, 8), :] = jnp.where(sub < STEPS, a, b)


def project(a, w):
    return pl.pallas_call(
        project_kernel,
        out_shape=jax.ShapeDtypeStruct((128, 128), F32),
        in_specs=[VM] * 2,
        out_specs=VM,
        compiler_params=LIMIT,
        cost_estimate=pl.CostEstimate(
            flops=270_000_000, transcendentals=0, bytes_accessed=2_000_000
        ),
    )(a, w)


def order_kernel(own_ref, other_ref, out_ref):
    first = (lax.axis_index("req") & 1) == 0
    mine, theirs = own_ref[...], other_ref[...]
    even = jnp.where(first, mine, theirs)
    odd = jnp.where(first, theirs, mine)
    sub = iota((8, 128), 0)
    for k in range(16):
        a, b = even[k * 8 : k * 8 + 8], odd[k * 8 : k * 8 + 8]
        out_ref[pl.ds(k * 16, 8), :] = jnp.where(sub < STEPS, a, pltpu.roll(b, STEPS, 0))
        out_ref[pl.ds(k * 16 + 8, 8), :] = jnp.where(sub < STEPS, pltpu.roll(a, STEPS, 0), b)


def in_order(own, other):
    return pl.pallas_call(
        order_kernel,
        out_shape=jax.ShapeDtypeStruct((REQS * STEPS, 128), F32),
        in_specs=[VM] * 2,
        out_specs=VM,
        compiler_params=LIMIT,
        name="in_order",
    )(own, other)


def over_chips(x):
    return lax.all_to_all(
        x, "req", split_axis=0, concat_axis=0, axis_index_groups=SAME_CORE, tiled=True
    )


def swap_cores(x):
    return lax.ppermute(x, "req", CORE_SWAP)


def local(queries, nk, nv, pk, pv, hk, hv, kept, membership, out_weight):
    packed, own = pack(membership, queries)
    pk1, pv1, w1 = swap_cores(pk), swap_cores(pv), swap_cores(out_weight)
    q = over_chips(packed)
    po, pll = private(own, kept, hk, hv, nk, nv)
    q, po, pll, w1 = lax.optimization_barrier((q, po, pll, w1))
    parts = over_chips(prefix(q, pk, pv, pk1, pv1))
    att = over_chips(combine(parts, po, pll))
    att = att.reshape(256, 2048)
    other = swap_cores(project(att, w1))
    part = in_order(project(att, out_weight), other)
    theirs = lax.ppermute(part, "kvh", [(0, 1), (1, 0)])
    return (part + theirs).astype(BF).reshape(REQS, STEPS, 128)


def solution(mesh):
    placed = (
        P("req", None, "kvh"),
        P("req", None, "kvh"),
        P("req", None, "kvh"),
        P(None, "req", "kvh"),
        P(None, "req", "kvh"),
        P("req", None, "kvh"),
        P("req", None, "kvh"),
        P("req", "kvh", None),
        P("req", None),
        P("kvh", "req"),
    )
    return jax.shard_map(
        local, mesh=mesh, in_specs=placed, out_specs=P(None, None, "req"), check_vma=False
    )
```
